256 devices in a mesh: dp: 32 (over z_hi, y, x), tensor: 8 (over z_lo, core).
Axes of the slice: x: 4, y: 4, z: 8 (z_hi: 2, z_lo: 4; z = z_hi * 4 + z_lo), core: 2. Of those that a mesh axis runs over, the one named last changes fastest.
Arguments:
- queries: bfloat16 [32768, 3072], P('dp', 'tensor'), may hold values from -70 to 70
- keys: bfloat16 [32768, 3072], P('dp', 'tensor'), may hold values from -5 to 5
- values: bfloat16 [32768, 3072], P('dp', 'tensor'), may hold values from -6 to 6
- out_gradient: bfloat16 [32768, 5120], P(('dp', 'tensor')), may hold values from -24 to 24
- out_weight: bfloat16 [3072, 5120], P('tensor'), may hold values from -0.109375 to 0.109375
- segments: int32 [32, 8], replicated, may hold values from 0 to 7, as said below
- counts: int32 [32], replicated, may hold values from 1 to 4, as said below
Outputs:
- query_gradient: bfloat16 [32768, 3072], P('dp', 'tensor')
- key_gradient: bfloat16 [32768, 3072], P('dp', 'tensor')
- value_gradient: bfloat16 [32768, 3072], P('dp', 'tensor')
- weight_gradient: float32 [5120, 3072], P('dp', 'tensor')
The draws below stay inside these ranges and needn't reach their ends.
Inputs may be any that keep to these rules, and one draw needn't show every extreme that they name: `segments`: along each row ids never fall; each protein spans 1 to 4 consecutive blocks, and some protein spans exactly 4; the last counts[r] blocks of replica r are whole proteins. counts[r] equals counts[(r + 16) mod 32].
All inputs are finite; a program needn't handle non-finite values.
Results may differ from the reference program's by a relative error of at most 0.025.
Values may be sent and summed in bfloat16 or wider, within the bound.
No kernel may reach another device: no remote copies, remote signals or barrier semaphores. Data moves between devices by JAX's collectives and lax.ppermute only.
A program may use at most 128 MiB of HBM per device.

```python
import jax
import jax.numpy as jnp
from jax import lax

D = 5120
HEADS = 24
HEAD_SIZE = 128
BLOCK = 128
BLOCKS = 8
MOVABLE = 4
INNER = 3072
REPLICAS = 32
REPLICA_ROWS = 1024
ROWS = 32768


def base_keys(key):
    raw = jnp.clip(jax.random.normal(jax.random.fold_in(key, 11), (ROWS, INNER), jnp.float32), -5.0, 5.0)
    return raw


def draw_keys(key, part):
    raw = base_keys(key)
    return raw.astype(jnp.bfloat16)


def draw_queries(key, part):
    raw = jnp.clip(jax.random.normal(jax.random.fold_in(key, 12), (ROWS, INNER), jnp.float32), -5.0, 5.0)
    return raw.astype(jnp.bfloat16)


def plan_tables(key):
    base = jax.random.fold_in(key, 21)
    pairs = REPLICAS // 2
    moves = jax.random.randint(jax.random.fold_in(base, 1), (pairs,), 1, MOVABLE + 1)
    moves = moves.at[1].set(1).at[0].set(MOVABLE)
    heavy_upper = jax.random.randint(jax.random.fold_in(base, 2), (pairs,), 0, 2)
    wanted = jax.random.randint(jax.random.fold_in(base, 3), (REPLICAS, BLOCKS), 0, 2)
    moved = jnp.concatenate([moves, moves])
    heavy = jnp.concatenate([1 - heavy_upper, heavy_upper])
    column = jnp.arange(BLOCKS)[None, :]
    boundary = BLOCKS - moved[:, None]
    in_tail = column >= boundary
    tail_start = jnp.where(heavy[:, None] == 1, column == boundary, True)
    head_start = (wanted == 1) | (column == 0)

    def advance(run, items):
        tail_here, tail_begin, head_begin = items
        begin = jnp.where(tail_here, tail_begin, head_begin | (run >= MOVABLE))
        return (jnp.where(begin, 1, run + 1), begin)
    final_run, begins = lax.scan(advance, jnp.zeros((REPLICAS,), jnp.int32), (in_tail.T, tail_start.T, head_start.T))
    protein_ids = jnp.cumsum(begins.T.astype(jnp.int32), axis=1) - 1
    return (protein_ids.astype(jnp.int32), moved.astype(jnp.int32))


def draw_segments(key, part):
    return plan_tables(key)[0]


def draw_counts(key, part):
    return plan_tables(key)[1]


def with_spikes(values, stream_key, source, target, shards_of, factor):
    owner, partner = [(jnp.arange(values.shape[axis_at]) // (values.shape[axis_at] // shards_of)).reshape([-1 if axis == axis_at else 1 for axis in range(values.ndim)]) for axis_at in (source, target)]
    chosen = jax.random.permutation(stream_key, shards_of)[partner]
    strong = (owner == chosen) | (owner == (partner + shards_of // 2) % shards_of)
    return jnp.where(strong, factor * values, values)


def block_scale(stream_key, dims, pieces, least, top_value):
    factor_of = 1.0
    for dim, parts in pieces:
        heights = jax.random.uniform(jax.random.fold_in(jax.random.fold_in(stream_key, 6), dim), (parts,), jnp.float32, least / len(pieces), top_value / len(pieces))
        factor_of = factor_of * jnp.repeat(jnp.exp(heights), dims[dim] // parts).reshape((-1,) + (1,) * (len(dims) - 1 - dim))
    return factor_of


def scatter_about(key, shape, spread, most, split=(), kind=jnp.bfloat16):
    factor_of = block_scale(key, shape, split, -0.22, 0.18) if split else 1.0
    drawn = jax.random.normal(key, shape, jnp.float32) * spread * factor_of
    return jnp.minimum(jnp.maximum(drawn, -most), most).astype(kind)


def gaussian_with(stream_key, dims, scale, reach, cuts, heavy, kind=jnp.bfloat16):
    entries = scale * jax.random.normal(stream_key, dims, jnp.float32)
    if cuts:
        entries = entries * block_scale(stream_key, dims, cuts, -0.22, 0.18)
    return jnp.clip(with_spikes(entries, jax.random.fold_in(stream_key, 3), *heavy), -reach, reach).astype(kind)


def setup_inputs(seed: int = 0) -> dict:
    key_list = jax.random.split(jax.random.key(seed), 8)
    return {
        "queries": draw_queries(jax.random.fold_in(key_list[7], 71), 0),
        "keys": draw_keys(jax.random.fold_in(key_list[7], 71), 0),
        "values": scatter_about(key_list[2], (ROWS, INNER), 1.0, 6.0, ((0, 32), (1, 8))),
        "out_gradient": gaussian_with(key_list[3], (ROWS, D), 1.0, 24.0, ((0, 256),), (0, 1, 256, 6.0)),
        "out_weight": scatter_about(key_list[4], (INNER, D), INNER ** -0.5, 0.109375, ((0, 8),)),
        "segments": draw_segments(jax.random.fold_in(key_list[7], 71), 0),
        "counts": draw_counts(jax.random.fold_in(key_list[7], 71), 0),
    }


masked_score = -1.0e30


def replica_backward(query, key_rows, value, gradient, seg_row):
    length = query.shape[0]
    scale = HEAD_SIZE ** -0.5
    protein = jnp.repeat(seg_row, BLOCK)
    matching = protein[:, None] == protein[None, :]
    query_heads = query.reshape(length, HEADS, HEAD_SIZE).astype(jnp.float32)
    key_heads = key_rows.reshape(length, HEADS, HEAD_SIZE).astype(jnp.float32)
    value_heads = value.reshape(length, HEADS, HEAD_SIZE).astype(jnp.float32)
    grad_heads = gradient.reshape(length, HEADS, HEAD_SIZE).astype(jnp.float32)
    scores = jnp.einsum("qhd,khd->hqk", query_heads, key_heads) * scale
    scores = jnp.where(matching[None], scores, masked_score)
    highest = jnp.max(scores, axis=2, keepdims=True)
    weights = jnp.exp(scores - highest)
    chances = weights / jnp.sum(weights, axis=2, keepdims=True)
    chance_weights = lax.optimization_barrier(chances.astype(jnp.bfloat16)).astype(jnp.float32)
    head_output = jnp.einsum("hqk,khd->qhd", chance_weights, value_heads).astype(jnp.bfloat16)
    output_wide = lax.optimization_barrier(head_output).astype(jnp.float32)
    centering = jnp.sum(grad_heads * output_wide, axis=2)
    chance_gradient = jnp.einsum("qhd,khd->hqk", grad_heads, value_heads)
    score_gradient = chances * (chance_gradient - jnp.transpose(centering)[:, :, None])
    score_gradient = lax.optimization_barrier(score_gradient.astype(jnp.bfloat16)).astype(jnp.float32)
    query_local = (jnp.einsum("hqk,khd->qhd", score_gradient, key_heads) * scale).astype(jnp.bfloat16)
    key_local = (jnp.einsum("hqk,qhd->khd", score_gradient, query_heads) * scale).astype(jnp.bfloat16)
    value_local = jnp.einsum("hqk,qhd->khd", chance_weights, grad_heads).astype(jnp.bfloat16)
    return (query_local.reshape(length, INNER), key_local.reshape(length, INNER),
            value_local.reshape(length, INNER), head_output.reshape(length, INNER))


def by_replica(items):
    return replica_backward(items[0], items[1], items[2], items[3], items[4])


def reference(queries, keys, values, out_gradient, out_weight, segments, counts):
    head_gradient = lax.dot_general(out_gradient, out_weight, (((1,), (1,)), ((), ())),
                                    preferred_element_type=jnp.float32).astype(jnp.bfloat16)

    def shaped(array):
        return array.reshape(REPLICAS, REPLICA_ROWS, INNER)

    query_local, key_local, value_local, head_output = lax.map(
        by_replica, (shaped(queries), shaped(keys), shaped(values), shaped(head_gradient), segments))
    output_flat = head_output.reshape(ROWS, INNER)
    weight_gradient = lax.dot_general(out_gradient, output_flat, (((0,), (0,)), ((), ())),
                                      preferred_element_type=jnp.float32) / REPLICAS
    moved = jnp.arange(BLOCKS, dtype=jnp.int32)[None, :] >= (BLOCKS - counts)[:, None]

    def settle(array):
        blocked = array.reshape(REPLICAS, BLOCKS, BLOCK, INNER)
        partner = jnp.roll(blocked, REPLICAS // 2, axis=0)
        return jnp.where(moved[:, :, None, None], partner, blocked).reshape(ROWS, INNER)

    return settle(query_local), settle(key_local), settle(value_local), weight_gradient
```

```python
import functools

import jax
import jax.numpy as jnp
from jax import lax
from jax.experimental import pallas as pl
from jax.experimental.pallas import tpu as pltpu
from jax.sharding import Mesh
from jax.sharding import PartitionSpec as P

HEAD_SIZE = 128
BLOCK = 128
WINDOW = 4
MOVABLE = 4
SCALE = HEAD_SIZE**-0.5
LOG2E = 1.4426950408889634
DP = ("z_hi", "y", "x")
TENSOR = ("z_lo", "core")
AXES = DP + TENSOR

masked_score = -1e30


def swapped(x, axis):
    n = lax.axis_size(axis)
    return lax.ppermute(x, axis, [(i, (i + n // 2) % n) for i in range(n)])


def dot(a, b, over):
    return lax.dot_general(
        a, b, (((over[0],), (over[1],)), ((), ())), preferred_element_type=jnp.float32
    )


def cost(flops, moved, transcendentals=0):
    return pl.CostEstimate(flops=flops, bytes_accessed=moved, transcendentals=transcendentals)


def window_of(ids, row, b):
    blocks = ids.shape[1]
    own = ids[row, b]
    first = jnp.int32(0)
    for j in range(blocks):
        first = first + jnp.where(ids[row, j] < own, 1, 0)
    start = jnp.minimum(first, blocks - WINDOW)
    return own, start, pl.ds(pl.multiple_of(start * BLOCK, BLOCK), WINDOW * BLOCK)


def forward_kernel(row_ref, ids_ref, q_ref, k_ref, v_ref, p_ref, o_ref):
    row = row_ref[0]
    for b in range(ids_ref.shape[1]):
        own, start, near = window_of(ids_ref, row, b)
        rows = pl.ds(b * BLOCK, BLOCK)
        scores = dot(q_ref[rows, :], k_ref[near, :], (1, 1))
        tiles = []
        for t in range(WINDOW):
            off = jnp.where(ids_ref[row, start + t] == own, 0.0, masked_score)
            tiles.append(scores[:, t * BLOCK : (t + 1) * BLOCK] + off)
        top = jnp.max(functools.reduce(jnp.maximum, tiles), axis=1, keepdims=True)
        tiles = [jnp.exp2((x - top) * (SCALE * LOG2E)) for x in tiles]
        total = jnp.sum(functools.reduce(jnp.add, tiles), axis=1, keepdims=True)
        inverse = 1.0 / total
        p = jnp.concatenate([(x * inverse).astype(jnp.bfloat16) for x in tiles], axis=1)
        p_ref[0, rows, :] = p
        o_ref[rows, :] = dot(p, v_ref[near, :], (1, 0)).astype(jnp.bfloat16)


def backward_kernel(
    row_ref, ids_ref, q_ref, k_ref, v_ref, g_ref, o_ref, p_ref,
    qf_ref, kf_ref, vf_ref, tail_ref, ka, va,
):
    row = row_ref[0]
    front = qf_ref.shape[0]
    ka[...] = jnp.zeros_like(ka)
    va[...] = jnp.zeros_like(va)
    for b in range(ids_ref.shape[1]):
        _, _, near = window_of(ids_ref, row, b)
        rows = pl.ds(b * BLOCK, BLOCK)
        g = g_ref[rows, :]
        p = p_ref[0, rows, :]
        dp = dot(g, v_ref[near, :], (1, 1))
        center = jnp.sum(
            g.astype(jnp.float32) * o_ref[rows, :].astype(jnp.float32), axis=1, keepdims=True
        )
        ds = (p.astype(jnp.float32) * (dp - center)).astype(jnp.bfloat16)
        dq = (dot(ds, k_ref[near, :], (1, 0)) * SCALE).astype(jnp.bfloat16)
        if b * BLOCK < front:
            qf_ref[rows, :] = dq
        else:
            tail_ref[0, pl.ds(b * BLOCK - front, BLOCK), :] = dq
        ka[near, :] += dot(ds, q_ref[rows, :], (0, 0))
        va[near, :] += dot(p, g, (0, 0))
    kf_ref[...] = (ka[:front] * SCALE).astype(jnp.bfloat16)
    tail_ref[1] = (ka[front:] * SCALE).astype(jnp.bfloat16)
    vf_ref[...] = va[:front].astype(jnp.bfloat16)
    tail_ref[2] = va[front:].astype(jnp.bfloat16)


def head_spec(rows):
    return pl.BlockSpec((rows, HEAD_SIZE), lambda h, *_: (0, h))


def forward(row, ids, q, k, v):
    rows, inner = q.shape
    heads = inner // HEAD_SIZE
    keys = WINDOW * BLOCK
    hs = head_spec(rows)
    return pl.pallas_call(
        forward_kernel,
        grid_spec=pltpu.PrefetchScalarGridSpec(
            num_scalar_prefetch=2,
            grid=(heads,),
            in_specs=[hs] * 3,
            out_specs=[pl.BlockSpec((1, rows, keys), lambda h, *_: (h, 0, 0)), hs],
        ),
        out_shape=[
            jax.ShapeDtypeStruct((heads, rows, keys), jnp.bfloat16),
            jax.ShapeDtypeStruct((rows, inner), jnp.bfloat16),
        ],
        cost_estimate=cost(4 * rows * keys * inner, 8 * rows * inner + 2 * heads * rows * keys, heads * rows * keys),
        name="forward",
    )(row, ids, q, k, v)


def backward(row, ids, q, k, v, g, o, p):
    rows, inner = q.shape
    heads = inner // HEAD_SIZE
    keys = WINDOW * BLOCK
    moving = MOVABLE * BLOCK
    hs = head_spec(rows)
    fs = head_spec(rows - moving)
    return pl.pallas_call(
        backward_kernel,
        grid_spec=pltpu.PrefetchScalarGridSpec(
            num_scalar_prefetch=2,
            grid=(heads,),
            in_specs=[hs] * 5 + [pl.BlockSpec((1, rows, keys), lambda h, *_: (h, 0, 0))],
            out_specs=[fs] * 3 + [pl.BlockSpec((3, moving, HEAD_SIZE), lambda h, *_: (0, 0, h))],
            scratch_shapes=[pltpu.VMEM((rows, HEAD_SIZE), jnp.float32)] * 2,
        ),
        out_shape=[jax.ShapeDtypeStruct((rows - moving, inner), jnp.bfloat16)] * 3
        + [jax.ShapeDtypeStruct((3, moving, inner), jnp.bfloat16)],
        cost_estimate=cost(8 * rows * keys * inner, 16 * rows * inner + 2 * heads * rows * keys),
        name="backward",
    )(row, ids, q, k, v, g, o, p)


def project_kernel(place_ref, own_ref, other_ref, w_ref, *rest):
    out_ref, acc = rest[-2:]
    step = pl.program_id(0)
    part = dot(jnp.concatenate([own_ref[...], other_ref[...]], axis=0), w_ref[...], (1, 1))

    @pl.when(step == 0)
    def _():
        acc[...] = part

    @pl.when(step > 0)
    def _():
        acc[...] += part

    @pl.when(step == pl.num_programs(0) - 1)
    def _():
        piece = own_ref.shape[0]
        core = place_ref[1]
        out_ref[pl.ds(pl.multiple_of(core * piece, piece), piece), :] = acc[:piece].astype(jnp.bfloat16)
        out_ref[pl.ds(pl.multiple_of((1 - core) * piece, piece), piece), :] = acc[piece:].astype(jnp.bfloat16)


def project(place, own, other, w, rows, before):
    piece, depth = own.shape
    inner = w.shape[0]
    width = 1024
    gs = pl.BlockSpec((piece, width), lambda j, *_: (0, j))
    in_specs = [gs, gs, pl.BlockSpec((inner, width), lambda j, *_: (0, j))]
    operands = [own, other, w]
    aliases = {}
    if before is not None:
        in_specs.append(pl.BlockSpec(memory_space=pl.ANY))
        operands.append(before)
        aliases = {4: 0}
    return pl.pallas_call(
        project_kernel,
        grid_spec=pltpu.PrefetchScalarGridSpec(
            num_scalar_prefetch=1,
            grid=(depth // width,),
            in_specs=in_specs,
            out_specs=pl.BlockSpec((2 * piece, inner), lambda j, place: (place[0], 0)),
            scratch_shapes=[pltpu.VMEM((2 * piece, inner), jnp.float32)],
        ),
        out_shape=jax.ShapeDtypeStruct((rows, inner), jnp.bfloat16),
        input_output_aliases=aliases,
        cost_estimate=cost(4 * piece * depth * inner, 4 * piece * depth + 2 * inner * depth),
        name="project",
    )(place, *operands)


def weight_kernel(order_ref, *refs):
    pieces, h_ref, out_ref, h_own = refs[:-3], refs[-3], refs[-2], refs[-1]
    piece = pieces[0].shape[0]

    @pl.when(pl.program_id(0) == 0)
    def _():
        for i in range(len(pieces)):
            at = pl.ds(pl.multiple_of(order_ref[i] * piece, piece), piece)
            h_own[i * piece : (i + 1) * piece, :] = h_ref[at, :]

    g = jnp.concatenate([ref[...] for ref in pieces], axis=0)
    out_ref[...] = (dot(g, h_own[...], (0, 0)) * (1.0 / 32)).astype(jnp.bfloat16)


def weight(order, pieces, h):
    rows, inner = h.shape
    piece, depth = pieces[0].shape
    width = 640
    return pl.pallas_call(
        weight_kernel,
        grid_spec=pltpu.PrefetchScalarGridSpec(
            num_scalar_prefetch=1,
            grid=(depth // width,),
            in_specs=[pl.BlockSpec((piece, width), lambda j, *_: (0, j))] * len(pieces)
            + [pl.BlockSpec((rows, inner), lambda j, *_: (0, 0))],
            out_specs=pl.BlockSpec((width, inner), lambda j, *_: (j, 0)),
            scratch_shapes=[pltpu.VMEM((rows, inner), jnp.bfloat16)],
        ),
        out_shape=jax.ShapeDtypeStruct((depth, inner), jnp.bfloat16),
        cost_estimate=cost(2 * rows * depth * inner, 2 * rows * depth + 2 * depth * inner),
        name="weight",
    )(order, *pieces, h)


def shards(queries, keys, values, out_gradient, out_weight, segments, counts):
    rows = queries.shape[0]
    blocks = segments.shape[1]
    block_rows = rows // blocks
    trailing = MOVABLE * block_rows
    chips = lax.axis_size("z_lo")
    chip = lax.axis_index("z_lo")
    core = lax.axis_index("core")
    position = lax.axis_index(DP)
    row = jnp.reshape(position, (1,)).astype(jnp.int32)

    chances, head_output = forward(row, segments, queries, keys, values)

    ring = [(i, (i + 1) % chips) for i in range(chips)]
    mine = out_gradient
    pieces, order, gradient = [], [], None
    for step in range(chips):
        if step:
            mine = lax.ppermute(mine, "z_lo", ring)
        other = swapped(mine, "core")
        source = (chip - step) % chips
        pieces += [mine, other]
        order += [source * 2 + core, source * 2 + 1 - core]
        place = jnp.stack([source, core]).astype(jnp.int32)
        gradient = project(place, mine, other, out_weight, rows, gradient)
    order = jnp.stack(order).astype(jnp.int32)

    *front, tail = backward(row, segments, queries, keys, values, gradient, head_output, chances)
    arrived = swapped(tail, "z_hi")
    moving = lax.dynamic_index_in_dim(counts, position, 0, keepdims=False)
    block_moved = jnp.arange(blocks, dtype=jnp.int32) >= blocks - moving
    row_moved = jnp.repeat(block_moved, block_rows)[-trailing:, None]
    settled = [
        jnp.concatenate([front[i], jnp.where(row_moved, arrived[i], tail[i])], axis=0)
        for i in range(3)
    ]

    total = weight(order, pieces, head_output)
    halves = []
    total = total.reshape(2, 16, -1, total.shape[1])
    for half in range(2):
        parts = lax.all_to_all(total[half], ("y", "x"), 0, 0, tiled=True)
        halves.append(jnp.sum(parts.astype(jnp.float32), axis=0))
    upper = lax.axis_index("z_hi") == 1
    kept = jnp.where(upper, halves[1], halves[0])
    sent = jnp.where(upper, halves[0], halves[1]).astype(jnp.bfloat16)
    weight_gradient = kept + swapped(sent, "z_hi").astype(jnp.float32)
    return (*settled, weight_gradient)


def solution(mesh):
    split = Mesh(mesh.devices.reshape(2, 4, 4, 4, 2), AXES)
    placed = (
        P(DP, TENSOR),
        P(DP, TENSOR),
        P(DP, TENSOR),
        P(AXES, None),
        P(TENSOR, None),
        P(),
        P(),
    )
    return jax.shard_map(
        shards,
        mesh=split,
        in_specs=placed,
        out_specs=(P(DP, TENSOR), P(DP, TENSOR), P(DP, TENSOR), P(DP, TENSOR)),
        check_vma=False,
    )
```

```python
import functools

import jax
import jax.numpy as jnp
from jax import lax
from jax.experimental import pallas as pl
from jax.experimental.pallas import tpu as pltpu
from jax.sharding import Mesh
from jax.sharding import PartitionSpec as P


HEAD_SIZE = 128
BLOCK = 128
WINDOW = 4
MOVABLE = 4
CHIPS = 4
REPLICAS = 32
SCALE = HEAD_SIZE**-0.5
LOG2E = 1.4426950408889634
DP = ("z_hi", "y", "x")
TENSOR = ("z_lo", "core")
AXES = DP + TENSOR

masked_score = -1e30


def swapped(x, axis):
    n = lax.axis_size(axis)
    return lax.ppermute(x, axis, [(i, (i + n // 2) % n) for i in range(n)])


def dot(a, b, over):
    return lax.dot_general(
        a, b, (((over[0],), (over[1],)), ((), ())), preferred_element_type=jnp.float32
    )


def cost(flops, moved, transcendentals=0):
    return pl.CostEstimate(flops=flops, bytes_accessed=moved, transcendentals=transcendentals)


def block_at(index, size=BLOCK):
    return pl.ds(pl.multiple_of(index * size, size), size)


def window_of(ids, row, b):
    blocks = ids.shape[1]
    own = ids[row, b]
    first = jnp.int32(0)
    for j in range(blocks):
        first = first + jnp.where(ids[row, j] < own, 1, 0)
    start = jnp.minimum(first, blocks - WINDOW)
    return own, start, pl.ds(pl.multiple_of(start * BLOCK, BLOCK), WINDOW * BLOCK)


def forward_kernel(here_ref, ids_ref, q_ref, k_ref, v_ref, p_ref, o_ref, r_ref):
    row, chip, core = here_ref[0], here_ref[1], here_ref[2]
    for b in range(ids_ref.shape[1]):
        own, start, near = window_of(ids_ref, row, b)
        rows = pl.ds(b * BLOCK, BLOCK)
        scores = dot(q_ref[rows, :], k_ref[near, :], (1, 1))
        tiles = []
        for t in range(WINDOW):
            off = jnp.where(ids_ref[row, start + t] == own, 0.0, masked_score)
            tiles.append(scores[:, t * BLOCK : (t + 1) * BLOCK] + off)
        top = jnp.max(functools.reduce(jnp.maximum, tiles), axis=1, keepdims=True)
        tiles = [jnp.exp2((x - top) * (SCALE * LOG2E)) for x in tiles]
        total = jnp.sum(functools.reduce(jnp.add, tiles), axis=1, keepdims=True)
        inverse = 1.0 / total
        p = jnp.concatenate([(x * inverse).astype(jnp.bfloat16) for x in tiles], axis=1)
        p_ref[0, rows, :] = p
        o = dot(p, v_ref[near, :], (1, 0)).astype(jnp.bfloat16)
        o_ref[rows, :] = o
        turn = lax.rem(chip + CHIPS - b // 2, CHIPS)
        r_ref[block_at(2 * turn + jnp.where(core == b % 2, 0, 1)), :] = o


def backward_kernel(
    here_ref, ids_ref, q_ref, k_ref, v_ref, g_ref, o_ref, p_ref,
    dq_ref, dk_ref, dv_ref, tail_ref, ka, va,
):
    row = here_ref[0]
    front = dq_ref.shape[0] - tail_ref.shape[1]
    ka[...] = jnp.zeros_like(ka)
    va[...] = jnp.zeros_like(va)
    for b in range(ids_ref.shape[1]):
        _, _, near = window_of(ids_ref, row, b)
        rows = pl.ds(b * BLOCK, BLOCK)
        g = g_ref[rows, :]
        p = p_ref[0, rows, :]
        dp = dot(g, v_ref[near, :], (1, 1))
        center = jnp.sum(
            g.astype(jnp.float32) * o_ref[rows, :].astype(jnp.float32), axis=1, keepdims=True
        )
        ds = (p.astype(jnp.float32) * (dp - center)).astype(jnp.bfloat16)
        dq_ref[rows, :] = (dot(ds, k_ref[near, :], (1, 0)) * SCALE).astype(jnp.bfloat16)
        ka[near, :] += dot(ds, q_ref[rows, :], (0, 0))
        va[near, :] += dot(p, g, (0, 0))
    dk_ref[...] = (ka[...] * SCALE).astype(jnp.bfloat16)
    dv_ref[...] = va[...].astype(jnp.bfloat16)
    for i, ref in enumerate((dq_ref, dk_ref, dv_ref)):
        tail_ref[i] = ref[front:, :]


def settle_kernel(here_ref, counts_ref, *refs):
    arrived_ref, outs, sems = refs[3], refs[4:7], refs[7]
    moving = counts_ref[here_ref[0]]
    front = outs[0].shape[0] - arrived_ref.shape[1]

    def copy(i, b):
        return pltpu.make_async_copy(
            arrived_ref.at[i, pl.ds(b * BLOCK, BLOCK), :],
            outs[i].at[pl.ds(front + b * BLOCK, BLOCK), :],
            sems.at[i, b],
        )

    for b in range(MOVABLE):

        @pl.when(b >= MOVABLE - moving)
        def _():
            for i in range(3):
                copy(i, b).start()

    for b in range(MOVABLE):

        @pl.when(b >= MOVABLE - moving)
        def _():
            for i in range(3):
                copy(i, b).wait()


def room(mebibytes):
    return pltpu.CompilerParams(vmem_limit_bytes=mebibytes * 2**20)


def prefetched(scalars, grid, in_specs, out_specs, scratch_shapes=()):
    return pltpu.PrefetchScalarGridSpec(
        num_scalar_prefetch=scalars,
        grid=grid,
        in_specs=in_specs,
        out_specs=out_specs,
        scratch_shapes=scratch_shapes,
    )


ANY = pl.BlockSpec(memory_space=pl.ANY)


def forward(here, ids, q, k, v):
    rows, inner = q.shape
    heads = inner // HEAD_SIZE
    keys = WINDOW * BLOCK
    hs = pl.BlockSpec((rows, HEAD_SIZE), lambda h, *_: (0, h))
    out = jax.ShapeDtypeStruct((rows, inner), jnp.bfloat16)
    return pl.pallas_call(
        forward_kernel,
        grid_spec=prefetched(
            2, (heads,), [hs] * 3, [pl.BlockSpec((1, rows, keys), lambda h, *_: (h, 0, 0)), hs, hs]
        ),
        out_shape=[jax.ShapeDtypeStruct((heads, rows, keys), jnp.bfloat16), out, out],
        cost_estimate=cost(
            4 * rows * keys * inner,
            10 * rows * inner + 2 * heads * rows * keys,
            heads * rows * keys,
        ),
        compiler_params=room(20),
        name="forward",
    )(here, ids, q, k, v)


def backward(here, ids, q, k, v, g, o, p):
    rows, inner = q.shape
    heads = inner // HEAD_SIZE
    keys = WINDOW * BLOCK
    moving = MOVABLE * BLOCK
    hs = pl.BlockSpec((rows, HEAD_SIZE), lambda h, *_: (0, h))
    return pl.pallas_call(
        backward_kernel,
        grid_spec=prefetched(
            2,
            (heads,),
            [hs] * 5 + [pl.BlockSpec((1, rows, keys), lambda h, *_: (h, 0, 0))],
            [hs] * 3 + [pl.BlockSpec((3, moving, HEAD_SIZE), lambda h, *_: (0, 0, h))],
            [pltpu.VMEM((rows, HEAD_SIZE), jnp.float32)] * 2,
        ),
        out_shape=[jax.ShapeDtypeStruct((rows, inner), jnp.bfloat16)] * 3
        + [jax.ShapeDtypeStruct((3, moving, inner), jnp.bfloat16)],
        compiler_params=room(20),
        cost_estimate=cost(8 * rows * keys * inner, 19 * rows * inner + 2 * heads * rows * keys),
        name="backward",
    )(here, ids, q, k, v, g, o, p)


def settle(here, counts, local, arrived):
    return pl.pallas_call(
        settle_kernel,
        grid_spec=prefetched(
            2,
            (1,),
            [ANY] * 3 + [pl.BlockSpec(memory_space=pltpu.VMEM)],
            [ANY] * 3,
            [pltpu.SemaphoreType.DMA((3, MOVABLE))],
        ),
        out_shape=[jax.ShapeDtypeStruct(x.shape, x.dtype) for x in local],
        input_output_aliases={2 + i: i for i in range(3)},
        compiler_params=room(8),
        cost_estimate=cost(0, 4 * arrived.size),
        name="settle",
    )(here, counts, *local, arrived)


def project_kernel(last, here_ref, *refs):
    pieces, w_ref = refs[: 2 * CHIPS], refs[2 * CHIPS]
    out_ref, acc = refs[-2:]
    step = pl.program_id(0)
    part = dot(jnp.concatenate([ref[...] for ref in pieces], axis=0), w_ref[...], (1, 1))
    chained = len(refs) == 2 * CHIPS + 4

    @pl.when(step == 0)
    def _():
        acc[...] = refs[2 * CHIPS + 1][...] + part if chained else part

    @pl.when(step > 0)
    def _():
        acc[...] += part

    @pl.when(step == pl.num_programs(0) - 1)
    def _():
        if not last:
            out_ref[...] = acc[...]
            return
        chip, core = here_ref[1], here_ref[2]
        for i in range(2 * CHIPS):
            source = lax.rem(chip + CHIPS - i // 2, CHIPS)
            block = 2 * source + (core if i % 2 == 0 else 1 - core)
            out_ref[block_at(block), :] = acc[i * BLOCK : (i + 1) * BLOCK].astype(jnp.bfloat16)


def piece_specs(pieces, first, width):
    def spec(i):
        at = first // width if i < 2 else 0
        return pl.BlockSpec((pieces[i].shape[0], width), lambda j, *_: (0, at + j))

    return [spec(i) for i in range(len(pieces))]


def project(here, pieces, first, width, w, before, last):
    depth = pieces[2].shape[1]
    rows = sum(x.shape[0] for x in pieces)
    inner = w.shape[0]
    at = first // width
    whole = pl.BlockSpec((rows, inner), lambda j, *_: (0, 0))
    in_specs = piece_specs(pieces, first, width)
    in_specs.append(pl.BlockSpec((inner, width), lambda j, *_: (0, at + j)))
    operands = [*pieces, w]
    if before is not None:
        in_specs.append(whole)
        operands.append(before)
    return pl.pallas_call(
        functools.partial(project_kernel, last),
        grid_spec=prefetched(
            1, (depth // width,), in_specs, whole, [pltpu.VMEM((rows, inner), jnp.float32)]
        ),
        out_shape=jax.ShapeDtypeStruct((rows, inner), jnp.bfloat16 if last else jnp.float32),
        cost_estimate=cost(
            2 * rows * depth * inner, 2 * rows * depth + 2 * inner * depth + 8 * rows * inner
        ),
        compiler_params=room(30),
        name="project",
    )(here, *operands)


def weight_kernel(here_ref, *refs):
    pieces, h_ref, out_ref = refs[: 2 * CHIPS], refs[2 * CHIPS], refs[-1]
    g = jnp.concatenate([ref[...] for ref in pieces], axis=0)
    out_ref[...] = (dot(g, h_ref[...], (0, 0)) * (1.0 / REPLICAS)).astype(jnp.bfloat16)


def weight(here, pieces, first, width, h):
    depth = pieces[2].shape[1]
    rows, inner = h.shape
    in_specs = piece_specs(pieces, first, width)
    in_specs.append(pl.BlockSpec((rows, inner), lambda j, *_: (0, 0)))
    return pl.pallas_call(
        weight_kernel,
        grid_spec=prefetched(
            1,
            (depth // width,),
            in_specs,
            pl.BlockSpec((width, inner), lambda j, *_: (j, 0)),
        ),
        out_shape=jax.ShapeDtypeStruct((depth, inner), jnp.bfloat16),
        compiler_params=room(26),
        cost_estimate=cost(
            2 * rows * depth * inner, 2 * rows * depth + 2 * depth * inner + 2 * rows * inner
        ),
        name="weight",
    )(here, *pieces, h)


def after(x, *others):
    return lax.optimization_barrier((x, *others))[0]


def steps(queries, keys, values, out_gradient, out_weight, segments, counts):
    depth = out_gradient.shape[1]
    half = depth // 2
    here = jnp.stack([lax.axis_index(DP), lax.axis_index("z_lo"), lax.axis_index("core")])
    here = here.astype(jnp.int32)
    ring = [(i, (i + 1) % CHIPS) for i in range(CHIPS)]

    own = [lax.slice_in_dim(out_gradient, c * half, (c + 1) * half, axis=1) for c in range(2)]
    partner = swapped(out_gradient, "core")
    pieces = [[out_gradient, partner] for _ in range(2)]

    def turn(c, x):
        y = lax.ppermute(x, "z_lo", ring)
        z = swapped(y, "core")
        pieces[c] += [y, z]
        return y

    first = turn(0, own[0])
    second = turn(0, first)
    turn(0, second)
    x = after(own[1], second)
    for _ in range(3):
        x = turn(1, x)

    chances, head_output, output_turned = forward(here, segments, queries, keys, values)

    gradient = None
    for c in range(2):
        gradient = project(here, pieces[c], c * half, 1280, out_weight, gradient, c == 1)

    sums = []
    for c in range(2):
        term = weight(here, pieces[c], c * half, 1280, output_turned)
        tiles = term.reshape(16, -1, term.shape[1])
        tiles = lax.all_to_all(tiles, ("y", "x"), 0, 0, tiled=True)
        sums.append(jnp.sum(tiles.astype(jnp.float32), axis=0))
    upper = lax.axis_index("z_hi") == 1
    kept = jnp.where(upper, sums[1], sums[0])
    sent = jnp.where(upper, sums[0], sums[1]).astype(jnp.bfloat16)
    got = swapped(sent, "z_hi")
    weight_gradient = kept + got.astype(jnp.float32)

    *local, tail = backward(here, segments, queries, keys, values, gradient, head_output, chances)
    arrived = swapped(tail, "z_hi")
    local = settle(here, counts, local, arrived)
    return (*local, weight_gradient)


def solution(mesh):
    split = Mesh(mesh.devices.reshape(2, 4, 4, CHIPS, 2), AXES)
    placed = (
        P(DP, TENSOR),
        P(DP, TENSOR),
        P(DP, TENSOR),
        P(AXES, None),
        P(TENSOR, None),
        P(),
        P(),
    )
    return jax.shard_map(
        steps,
        mesh=split,
        in_specs=placed,
        out_specs=(P(DP, TENSOR), P(DP, TENSOR), P(DP, TENSOR), P(DP, TENSOR)),
        check_vma=False,
    )
```

```python
import functools

import jax
import jax.numpy as jnp
from jax import lax
from jax.experimental import pallas as pl
from jax.experimental.pallas import tpu as pltpu
from jax.sharding import Mesh
from jax.sharding import PartitionSpec as P


HEAD_SIZE = 128
BLOCK = 128
WINDOW = 4
MOVABLE = 4
CHIPS = 4
REPLICAS = 32
SCALE = HEAD_SIZE**-0.5
LOG2E = 1.4426950408889634
DP = ("z_hi", "y", "x")
TENSOR = ("z_lo", "core")
AXES = DP + TENSOR

masked_score = -1e30


def swapped(x, axis):
    n = lax.axis_size(axis)
    return lax.ppermute(x, axis, [(i, (i + n // 2) % n) for i in range(n)])


def dot(a, b, over):
    return lax.dot_general(
        a, b, (((over[0],), (over[1],)), ((), ())), preferred_element_type=jnp.float32
    )


def cost(flops, moved, transcendentals=0):
    return pl.CostEstimate(flops=flops, bytes_accessed=moved, transcendentals=transcendentals)


def block_at(index, size=BLOCK):
    return pl.ds(pl.multiple_of(index * size, size), size)


def window_of(ids, row, b):
    blocks = ids.shape[1]
    own = ids[row, b]
    first = jnp.int32(0)
    for j in range(blocks):
        first = first + jnp.where(ids[row, j] < own, 1, 0)
    start = jnp.minimum(first, blocks - WINDOW)
    return own, start, pl.ds(pl.multiple_of(start * BLOCK, BLOCK), WINDOW * BLOCK)


def forward_kernel(here_ref, ids_ref, q_ref, k_ref, v_ref, p_ref, o_ref, r_ref, kt_ref, vt):
    row, chip, core = here_ref[0], here_ref[1], here_ref[2]
    kt_ref[...] = k_ref[...].T
    vt[...] = v_ref[...].T
    for b in range(ids_ref.shape[1]):
        own, start, near = window_of(ids_ref, row, b)
        rows = pl.ds(b * BLOCK, BLOCK)
        scores = dot(k_ref[near, :], q_ref[rows, :], (1, 1))
        tiles = []
        for t in range(WINDOW):
            off = jnp.where(ids_ref[row, start + t] == own, 0.0, masked_score)
            tiles.append(scores[t * BLOCK : (t + 1) * BLOCK] + off)
        top = jnp.max(functools.reduce(jnp.maximum, tiles), axis=0, keepdims=True)
        tiles = [jnp.exp2((x - top) * (SCALE * LOG2E)) for x in tiles]
        total = jnp.sum(functools.reduce(jnp.add, tiles), axis=0, keepdims=True)
        inverse = 1.0 / total
        p = jnp.concatenate([(x * inverse).astype(jnp.bfloat16) for x in tiles], axis=0)
        p_ref[0, b] = p
        o = dot(vt[:, near], p, (1, 0)).T.astype(jnp.bfloat16)
        o_ref[rows, :] = o
        turn = lax.rem(chip + CHIPS - b // 2, CHIPS)
        r_ref[block_at(2 * turn + jnp.where(core == b % 2, 0, 1)), :] = o


def backward_kernel(
    here_ref, ids_ref, q_ref, kt_ref, v_ref, g_ref, o_ref, p_ref,
    dq_ref, dk_ref, dv_ref, tail_ref, ka, va,
):
    row = here_ref[0]
    front = dq_ref.shape[0] - tail_ref.shape[1]
    ka[...] = jnp.zeros_like(ka)
    va[...] = jnp.zeros_like(va)
    for b in range(ids_ref.shape[1]):
        _, _, near = window_of(ids_ref, row, b)
        rows = pl.ds(b * BLOCK, BLOCK)
        g = g_ref[rows, :]
        p = p_ref[0, b]
        dp = dot(v_ref[near, :], g, (1, 1))
        center = jnp.sum(
            (g.astype(jnp.float32) * o_ref[rows, :].astype(jnp.float32)).T, axis=0, keepdims=True
        )
        ds = (p.astype(jnp.float32) * (dp - center)).astype(jnp.bfloat16)
        dq_ref[rows, :] = (dot(kt_ref[:, near], ds, (1, 0)) * SCALE).T.astype(jnp.bfloat16)
        ka[near, :] += dot(ds, q_ref[rows, :], (1, 0))
        va[near, :] += dot(p, g, (1, 0))
    dk_ref[...] = (ka[...] * SCALE).astype(jnp.bfloat16)
    dv_ref[...] = va[...].astype(jnp.bfloat16)
    for i, ref in enumerate((dq_ref, dk_ref, dv_ref)):
        tail_ref[i] = ref[front:, :]


def settle_kernel(here_ref, counts_ref, *refs):
    arrived_ref, outs, sems = refs[3], refs[4:7], refs[7]
    moving = counts_ref[here_ref[0]]
    front = outs[0].shape[0] - arrived_ref.shape[1]

    def copy(i, b):
        return pltpu.make_async_copy(
            arrived_ref.at[i, pl.ds(b * BLOCK, BLOCK), :],
            outs[i].at[pl.ds(front + b * BLOCK, BLOCK), :],
            sems.at[i, b],
        )

    for b in range(MOVABLE):

        @pl.when(b >= MOVABLE - moving)
        def _():
            for i in range(3):
                copy(i, b).start()

    for b in range(MOVABLE):

        @pl.when(b >= MOVABLE - moving)
        def _():
            for i in range(3):
                copy(i, b).wait()


def room(mebibytes):
    return pltpu.CompilerParams(vmem_limit_bytes=mebibytes * 2**20)


def prefetched(scalars, grid, in_specs, out_specs, scratch_shapes=()):
    return pltpu.PrefetchScalarGridSpec(
        num_scalar_prefetch=scalars,
        grid=grid,
        in_specs=in_specs,
        out_specs=out_specs,
        scratch_shapes=scratch_shapes,
    )


ANY = pl.BlockSpec(memory_space=pl.ANY)


def forward(here, ids, q, k, v):
    rows, inner = q.shape
    heads, blocks = inner // HEAD_SIZE, rows // BLOCK
    keys = WINDOW * BLOCK
    hs = pl.BlockSpec((rows, HEAD_SIZE), lambda h, *_: (0, h))
    ps = pl.BlockSpec((1, blocks, keys, BLOCK), lambda h, *_: (h, 0, 0, 0))
    ts = pl.BlockSpec((HEAD_SIZE, rows), lambda h, *_: (h, 0))
    out = jax.ShapeDtypeStruct((rows, inner), jnp.bfloat16)
    return pl.pallas_call(
        forward_kernel,
        grid_spec=prefetched(
            2,
            (heads,),
            [hs] * 3,
            [ps, hs, hs, ts],
            [pltpu.VMEM((HEAD_SIZE, rows), jnp.bfloat16)],
        ),
        out_shape=[
            jax.ShapeDtypeStruct((heads, blocks, keys, BLOCK), jnp.bfloat16),
            out,
            out,
            jax.ShapeDtypeStruct((inner, rows), jnp.bfloat16),
        ],
        compiler_params=room(20),
        cost_estimate=cost(
            4 * rows * keys * inner,
            12 * rows * inner + 2 * heads * rows * keys,
            heads * rows * keys,
        ),
        name="forward",
    )(here, ids, q, k, v)


def backward(here, ids, q, kt, v, g, o, p):
    rows, inner = q.shape
    heads, blocks = inner // HEAD_SIZE, rows // BLOCK
    keys = WINDOW * BLOCK
    moving = MOVABLE * BLOCK
    hs = pl.BlockSpec((rows, HEAD_SIZE), lambda h, *_: (0, h))
    ps = pl.BlockSpec((1, blocks, keys, BLOCK), lambda h, *_: (h, 0, 0, 0))
    ts = pl.BlockSpec((HEAD_SIZE, rows), lambda h, *_: (h, 0))
    return pl.pallas_call(
        backward_kernel,
        grid_spec=prefetched(
            2,
            (heads,),
            [hs, ts, hs, hs, hs, ps],
            [hs] * 3 + [pl.BlockSpec((3, moving, HEAD_SIZE), lambda h, *_: (0, 0, h))],
            [pltpu.VMEM((rows, HEAD_SIZE), jnp.float32)] * 2,
        ),
        out_shape=[jax.ShapeDtypeStruct((rows, inner), jnp.bfloat16)] * 3
        + [jax.ShapeDtypeStruct((3, moving, inner), jnp.bfloat16)],
        compiler_params=room(20),
        cost_estimate=cost(8 * rows * keys * inner, 19 * rows * inner + 2 * heads * rows * keys),
        name="backward",
    )(here, ids, q, kt, v, g, o, p)


def settle(here, counts, local, arrived):
    return pl.pallas_call(
        settle_kernel,
        grid_spec=prefetched(
            2,
            (1,),
            [ANY] * 3 + [pl.BlockSpec(memory_space=pltpu.VMEM)],
            [ANY] * 3,
            [pltpu.SemaphoreType.DMA((3, MOVABLE))],
        ),
        out_shape=[jax.ShapeDtypeStruct(x.shape, x.dtype) for x in local],
        input_output_aliases={2 + i: i for i in range(3)},
        compiler_params=room(8),
        cost_estimate=cost(0, 4 * arrived.size),
        name="settle",
    )(here, counts, *local, arrived)


def project_kernel(turns, final, here_ref, *refs):
    count = 2 * len(turns)
    pieces, w_ref = refs[:count], refs[count]
    out_ref, acc = refs[-2:]
    step = pl.program_id(0)
    part = dot(jnp.concatenate([ref[...] for ref in pieces], axis=0), w_ref[...], (1, 1))

    @pl.when(step == 0)
    def _():
        acc[...] = refs[count + 1][...] + part if final else part

    @pl.when(step > 0)
    def _():
        acc[...] += part

    @pl.when(step == pl.num_programs(0) - 1)
    def _():
        if not final:
            out_ref[...] = acc[...]
            return
        chip, core = here_ref[1], here_ref[2]
        for i in range(count):
            block = core if i % 2 == 0 else 1 - core
            if len(turns) > 1:
                block += 2 * lax.rem(chip + CHIPS - turns[i // 2], CHIPS)
            out_ref[block_at(block), :] = acc[i * BLOCK : (i + 1) * BLOCK].astype(jnp.bfloat16)


def piece_specs(pieces, first, width):
    def spec(x):
        at = first // width if x.shape[1] > pieces[-1].shape[1] else 0
        return pl.BlockSpec((x.shape[0], width), lambda j, *_: (0, at + j))

    return [spec(x) for x in pieces]


def in_hbm(x):
    return pltpu.with_memory_space_constraint(x, pltpu.HBM)


def project(here, turns, pieces, first, width, w, partial, before):
    pieces = [x for t in turns for x in pieces[2 * t : 2 * t + 2]]
    depth = pieces[-1].shape[1]
    rows = sum(x.shape[0] for x in pieces)
    inner = w.shape[0]
    at, place = first // width, turns[0] * 2 * BLOCK // rows
    final = partial is not None
    in_specs = piece_specs(pieces, first, width)
    in_specs.append(pl.BlockSpec((inner, width), lambda j, *_: (0, at + j)))
    operands = [*pieces, in_hbm(w)]
    aliases = {}
    total = rows
    out_spec = pl.BlockSpec((rows, inner), lambda j, *_: (0, 0))
    if final:
        total = partial.shape[0]
        in_specs.append(pl.BlockSpec((rows, inner), lambda j, *_: (place, 0)))
        operands.append(partial)
        out_spec = pl.BlockSpec((total, inner), lambda j, *_: (0, 0))
    if before is not None:
        in_specs.append(ANY)
        operands.append(before)
        aliases = {len(operands): 0}
        out_spec = pl.BlockSpec(
            (rows, inner), lambda j, here: (lax.rem(here[1] + CHIPS - turns[0], CHIPS), 0)
        )
    return pl.pallas_call(
        functools.partial(project_kernel, turns, final),
        grid_spec=prefetched(
            1, (depth // width,), in_specs, out_spec, [pltpu.VMEM((rows, inner), jnp.float32)]
        ),
        out_shape=jax.ShapeDtypeStruct((total, inner), jnp.bfloat16 if final else jnp.float32),
        input_output_aliases=aliases,
        compiler_params=room(30),
        cost_estimate=cost(
            2 * rows * depth * inner, 2 * rows * depth + 2 * inner * depth + 8 * rows * inner
        ),
        name="project",
    )(here, *operands)


def weight_kernel(here_ref, *refs):
    pieces, h_ref, out_ref = refs[: 2 * CHIPS], refs[2 * CHIPS], refs[-1]
    g = jnp.concatenate([ref[...] for ref in pieces], axis=0)
    out_ref[...] = (dot(g, h_ref[...], (0, 0)) * (1.0 / REPLICAS)).astype(jnp.bfloat16)


def weight(here, pieces, first, width, h):
    depth = pieces[2].shape[1]
    rows, inner = h.shape
    in_specs = piece_specs(pieces, first, width)
    in_specs.append(pl.BlockSpec((rows, inner), lambda j, *_: (0, 0)))
    return pl.pallas_call(
        weight_kernel,
        grid_spec=prefetched(
            1,
            (depth // width,),
            in_specs,
            pl.BlockSpec((width, inner), lambda j, *_: (j, 0)),
        ),
        out_shape=jax.ShapeDtypeStruct((depth, inner), jnp.bfloat16),
        compiler_params=room(26),
        cost_estimate=cost(
            2 * rows * depth * inner, 2 * rows * depth + 2 * depth * inner + 2 * rows * inner
        ),
        name="weight",
    )(here, *pieces, h)


def after(x, *others):
    return lax.optimization_barrier((x, *others))[0]


def steps(queries, keys, values, out_gradient, out_weight, segments, counts):
    depth = out_gradient.shape[1]
    half = depth // 2
    here = jnp.stack([lax.axis_index(DP), lax.axis_index("z_lo"), lax.axis_index("core")])
    here = here.astype(jnp.int32)
    ring = [(i, (i + 1) % CHIPS) for i in range(CHIPS)]

    partner = swapped(out_gradient, "core")
    pieces = [[out_gradient, partner] for _ in range(2)]

    def turn(c, x):
        y = lax.ppermute(x, "z_lo", ring)
        z = swapped(y, "core")
        pieces[c] += [y, z]
        return y

    first = turn(0, lax.slice_in_dim(out_gradient, 0, half, axis=1))
    later = lax.slice_in_dim(after(out_gradient, first), half, depth, axis=1)
    second = turn(0, first)
    turn(0, second)
    x = after(later, second)
    for _ in range(3):
        x = turn(1, x)

    chances, head_output, output_turned, keys_turned = forward(here, segments, queries, keys, values)

    partial = project(here, (0, 1, 2, 3), pieces[0], 0, 1280, out_weight, None, None)
    gradient = project(here, (0, 1, 2), pieces[1], half, 1280, out_weight, partial, None)
    gradient = project(here, (3,), pieces[1], half, 1280, out_weight, partial, gradient)

    sums = []
    for c in range(2):
        term = weight(here, pieces[c], c * half, 1280, output_turned)
        tiles = term.reshape(16, -1, term.shape[1])
        tiles = lax.all_to_all(tiles, ("y", "x"), 0, 0, tiled=True)
        sums.append(jnp.sum(tiles.astype(jnp.float32), axis=0))
    upper = lax.axis_index("z_hi") == 1
    kept = jnp.where(upper, sums[1], sums[0])
    sent = jnp.where(upper, sums[0], sums[1]).astype(jnp.bfloat16)
    got = swapped(sent, "z_hi")
    weight_gradient = kept + got.astype(jnp.float32)

    *local, tail = backward(
        here, segments, queries, keys_turned, values, gradient, head_output, chances
    )
    arrived = swapped(tail, "z_hi")
    local = settle(here, counts, local, arrived)
    return (*local, weight_gradient)


def solution(mesh):
    split = Mesh(mesh.devices.reshape(2, 4, 4, CHIPS, 2), AXES)
    placed = (
        P(DP, TENSOR),
        P(DP, TENSOR),
        P(DP, TENSOR),
        P(AXES, None),
        P(TENSOR, None),
        P(),
        P(),
    )
    return jax.shard_map(
        steps,
        mesh=split,
        in_specs=placed,
        out_specs=(P(DP, TENSOR), P(DP, TENSOR), P(DP, TENSOR), P(DP, TENSOR)),
        check_vma=False,
    )
```

```python
import functools

import jax
import jax.numpy as jnp
from jax import lax
from jax.experimental import pallas as pl
from jax.experimental.pallas import tpu as pltpu
from jax.sharding import Mesh
from jax.sharding import PartitionSpec as P


HEAD_SIZE = 128
BLOCK = 128
WINDOW = 4
MOVABLE = 4
CHIPS = 4
REPLICAS = 32
SCALE = HEAD_SIZE**-0.5
LOG2E = 1.4426950408889634
DP = ("z_hi", "y", "x")
TENSOR = ("z_lo", "core")
AXES = DP + TENSOR

masked_score = -1e30


def swapped(x, axis):
    n = lax.axis_size(axis)
    return lax.ppermute(x, axis, [(i, (i + n // 2) % n) for i in range(n)])


def dot(a, b, over):
    return lax.dot_general(
        a, b, (((over[0],), (over[1],)), ((), ())), preferred_element_type=jnp.float32
    )


def cost(flops, moved, transcendentals=0):
    return pl.CostEstimate(flops=flops, bytes_accessed=moved, transcendentals=transcendentals)


def block_at(index, size=BLOCK):
    return pl.ds(pl.multiple_of(index * size, size), size)


def window_of(ids, row, b):
    blocks = ids.shape[1]
    own = ids[row, b]
    first = jnp.int32(0)
    for j in range(blocks):
        first = first + jnp.where(ids[row, j] < own, 1, 0)
    start = jnp.minimum(first, blocks - WINDOW)
    return own, start, pl.ds(pl.multiple_of(start * BLOCK, BLOCK), WINDOW * BLOCK)


def forward_kernel(here_ref, ids_ref, q_ref, k_ref, v_ref, p_ref, o_ref, r_ref, kt_ref, vt):
    row, chip, core = here_ref[0], here_ref[1], here_ref[2]
    kt_ref[...] = k_ref[...].T
    vt[...] = v_ref[...].T
    for b in range(ids_ref.shape[1]):
        own, start, near = window_of(ids_ref, row, b)
        rows = pl.ds(b * BLOCK, BLOCK)
        scores = dot(k_ref[near, :], q_ref[rows, :], (1, 1))
        tiles = []
        for t in range(WINDOW):
            off = jnp.where(ids_ref[row, start + t] == own, 0.0, masked_score)
            tiles.append(scores[t * BLOCK : (t + 1) * BLOCK] + off)
        top = jnp.max(functools.reduce(jnp.maximum, tiles), axis=0, keepdims=True)
        tiles = [jnp.exp2((x - top) * (SCALE * LOG2E)) for x in tiles]
        total = jnp.sum(functools.reduce(jnp.add, tiles), axis=0, keepdims=True)
        inverse = 1.0 / total
        p = jnp.concatenate([(x * inverse).astype(jnp.bfloat16) for x in tiles], axis=0)
        p_ref[0, b] = p
        o = dot(vt[:, near], p, (1, 0)).T.astype(jnp.bfloat16)
        o_ref[rows, :] = o
        turn = lax.rem(chip + CHIPS - b // 2, CHIPS)
        r_ref[block_at(2 * turn + jnp.where(core == b % 2, 0, 1)), :] = o


def backward_kernel(
    here_ref, ids_ref, q_ref, kt_ref, v_ref, g_ref, o_ref, p_ref, *rest
):
    dq_ref, dk_ref, dv_ref, tail_ref, ka, va = rest[-6:]
    row = here_ref[0]
    front = dq_ref.shape[0] - tail_ref.shape[1]
    ka[...] = jnp.zeros_like(ka)
    va[...] = jnp.zeros_like(va)
    for b in range(ids_ref.shape[1]):
        _, _, near = window_of(ids_ref, row, b)
        rows = pl.ds(b * BLOCK, BLOCK)
        g = g_ref[rows, :]
        p = p_ref[0, b]
        dp = dot(v_ref[near, :], g, (1, 1))
        center = jnp.sum(
            (g.astype(jnp.float32) * o_ref[rows, :].astype(jnp.float32)).T, axis=0, keepdims=True
        )
        ds = (p.astype(jnp.float32) * (dp - center)).astype(jnp.bfloat16)
        dq_ref[rows, :] = (dot(kt_ref[:, near], ds, (1, 0)) * SCALE).T.astype(jnp.bfloat16)
        ka[near, :] += dot(ds, q_ref[rows, :], (1, 0))
        va[near, :] += dot(p, g, (1, 0))
    dk_ref[...] = (ka[...] * SCALE).astype(jnp.bfloat16)
    dv_ref[...] = va[...].astype(jnp.bfloat16)
    for i, ref in enumerate((dq_ref, dk_ref, dv_ref)):
        tail_ref[i] = ref[front:, :]


def settle_kernel(column, here_ref, counts_ref, *refs):
    arrived_ref, outs, sems = refs[3], refs[4:7], refs[7]
    moving = counts_ref[here_ref[0]]
    front = outs[0].shape[0] - arrived_ref.shape[1]

    def copy(i, b):
        return pltpu.make_async_copy(
            arrived_ref.at[i, pl.ds(b * BLOCK, BLOCK), :],
            outs[i].at[pl.ds(front + b * BLOCK, BLOCK), pl.ds(column, arrived_ref.shape[2])],
            sems.at[i, b],
        )

    for b in range(MOVABLE):

        @pl.when(b >= MOVABLE - moving)
        def _():
            for i in range(3):
                copy(i, b).start()

    for b in range(MOVABLE):

        @pl.when(b >= MOVABLE - moving)
        def _():
            for i in range(3):
                copy(i, b).wait()


def room(mebibytes):
    return pltpu.CompilerParams(vmem_limit_bytes=mebibytes * 2**20)


def prefetched(scalars, grid, in_specs, out_specs, scratch_shapes=()):
    return pltpu.PrefetchScalarGridSpec(
        num_scalar_prefetch=scalars,
        grid=grid,
        in_specs=in_specs,
        out_specs=out_specs,
        scratch_shapes=scratch_shapes,
    )


ANY = pl.BlockSpec(memory_space=pl.ANY)


def forward(here, ids, q, k, v):
    rows, inner = q.shape
    heads, blocks = inner // HEAD_SIZE, rows // BLOCK
    keys = WINDOW * BLOCK
    hs = pl.BlockSpec((rows, HEAD_SIZE), lambda h, *_: (0, h))
    ps = pl.BlockSpec((1, blocks, keys, BLOCK), lambda h, *_: (h, 0, 0, 0))
    ts = pl.BlockSpec((HEAD_SIZE, rows), lambda h, *_: (h, 0))
    out = jax.ShapeDtypeStruct((rows, inner), jnp.bfloat16)
    return pl.pallas_call(
        forward_kernel,
        grid_spec=prefetched(
            2,
            (heads,),
            [hs] * 3,
            [ps, hs, hs, ts],
            [pltpu.VMEM((HEAD_SIZE, rows), jnp.bfloat16)],
        ),
        out_shape=[
            jax.ShapeDtypeStruct((heads, blocks, keys, BLOCK), jnp.bfloat16),
            out,
            out,
            jax.ShapeDtypeStruct((inner, rows), jnp.bfloat16),
        ],
        compiler_params=room(20),
        cost_estimate=cost(
            4 * rows * keys * inner,
            12 * rows * inner + 2 * heads * rows * keys,
            heads * rows * keys,
        ),
        name="forward",
    )(here, ids, q, k, v)


def backward(here, ids, first, heads, q, kt, v, g, o, p, before):
    rows, inner = q.shape
    blocks = rows // BLOCK
    keys = WINDOW * BLOCK
    moving = MOVABLE * BLOCK
    hs = pl.BlockSpec((rows, HEAD_SIZE), lambda h, *_: (0, first + h))
    ps = pl.BlockSpec((1, blocks, keys, BLOCK), lambda h, *_: (first + h, 0, 0, 0))
    ts = pl.BlockSpec((HEAD_SIZE, rows), lambda h, *_: (first + h, 0))
    return pl.pallas_call(
        backward_kernel,
        grid_spec=prefetched(
            2,
            (heads,),
            [hs, ts, hs, hs, hs, ps] + [ANY] * len(before),
            [hs] * 3 + [pl.BlockSpec((3, moving, HEAD_SIZE), lambda h, *_: (0, 0, h))],
            [pltpu.VMEM((rows, HEAD_SIZE), jnp.float32)] * 2,
        ),
        out_shape=[jax.ShapeDtypeStruct((rows, inner), jnp.bfloat16)] * 3
        + [jax.ShapeDtypeStruct((3, moving, heads * HEAD_SIZE), jnp.bfloat16)],
        input_output_aliases={8 + i: i for i in range(len(before))},
        compiler_params=room(20),
        cost_estimate=cost(
            8 * rows * keys * heads * HEAD_SIZE,
            19 * rows * heads * HEAD_SIZE + 2 * heads * rows * keys,
        ),
        name="backward",
    )(here, ids, q, kt, v, g, o, p, *before)


def settle(here, counts, first, local, arrived):
    return pl.pallas_call(
        functools.partial(settle_kernel, first * HEAD_SIZE),
        grid_spec=prefetched(
            2,
            (1,),
            [ANY] * 3 + [pl.BlockSpec(memory_space=pltpu.VMEM)],
            [ANY] * 3,
            [pltpu.SemaphoreType.DMA((3, MOVABLE))],
        ),
        out_shape=[jax.ShapeDtypeStruct(x.shape, x.dtype) for x in local],
        input_output_aliases={2 + i: i for i in range(3)},
        compiler_params=room(8),
        cost_estimate=cost(0, 4 * arrived.size),
        name="settle",
    )(here, counts, *local, arrived)


def project_kernel(turns, final, here_ref, *refs):
    count = 2 * len(turns)
    pieces, w_ref = refs[:count], refs[count]
    out_ref, acc = refs[-2:]
    step = pl.program_id(0)
    part = dot(jnp.concatenate([ref[...] for ref in pieces], axis=0), w_ref[...], (1, 1))

    @pl.when(step == 0)
    def _():
        acc[...] = refs[count + 1][...] + part if final else part

    @pl.when(step > 0)
    def _():
        acc[...] += part

    @pl.when(step == pl.num_programs(0) - 1)
    def _():
        if not final:
            out_ref[...] = acc[...]
            return
        chip, core = here_ref[1], here_ref[2]
        for i in range(count):
            block = core if i % 2 == 0 else 1 - core
            if len(turns) > 1:
                block += 2 * lax.rem(chip + CHIPS - turns[i // 2], CHIPS)
            out_ref[block_at(block), :] = acc[i * BLOCK : (i + 1) * BLOCK].astype(jnp.bfloat16)


def piece_specs(pieces, first, width):
    def spec(x):
        at = first // width if x.shape[1] > pieces[-1].shape[1] else 0
        return pl.BlockSpec((x.shape[0], width), lambda j, *_: (0, at + j))

    return [spec(x) for x in pieces]


def in_hbm(x):
    return pltpu.with_memory_space_constraint(x, pltpu.HBM)


def project(here, turns, pieces, first, width, w, partial, before):
    pieces = [x for t in turns for x in pieces[2 * t : 2 * t + 2]]
    depth = pieces[-1].shape[1]
    rows = sum(x.shape[0] for x in pieces)
    inner = w.shape[0]
    at, place = first // width, turns[0] * 2 * BLOCK // rows
    final = partial is not None
    in_specs = piece_specs(pieces, first, width)
    in_specs.append(pl.BlockSpec((inner, width), lambda j, *_: (0, at + j)))
    operands = [*pieces, in_hbm(w)]
    aliases = {}
    total = rows
    out_spec = pl.BlockSpec((rows, inner), lambda j, *_: (0, 0))
    if final:
        total = partial.shape[0]
        in_specs.append(pl.BlockSpec((rows, inner), lambda j, *_: (place, 0)))
        operands.append(partial)
        out_spec = pl.BlockSpec((total, inner), lambda j, *_: (0, 0))
    if before is not None:
        in_specs.append(ANY)
        operands.append(before)
        aliases = {len(operands): 0}
        out_spec = pl.BlockSpec(
            (rows, inner), lambda j, here: (lax.rem(here[1] + CHIPS - turns[0], CHIPS), 0)
        )
    return pl.pallas_call(
        functools.partial(project_kernel, turns, final),
        grid_spec=prefetched(
            1, (depth // width,), in_specs, out_spec, [pltpu.VMEM((rows, inner), jnp.float32)]
        ),
        out_shape=jax.ShapeDtypeStruct((total, inner), jnp.bfloat16 if final else jnp.float32),
        input_output_aliases=aliases,
        compiler_params=room(30),
        cost_estimate=cost(
            2 * rows * depth * inner, 2 * rows * depth + 2 * inner * depth + 8 * rows * inner
        ),
        name="project",
    )(here, *operands)


def weight_kernel(here_ref, *refs):
    pieces, h_ref, out_ref = refs[: 2 * CHIPS], refs[2 * CHIPS], refs[-1]
    g = jnp.concatenate([ref[...] for ref in pieces], axis=0)
    out_ref[...] = (dot(g, h_ref[...], (0, 0)) * (1.0 / REPLICAS)).astype(jnp.bfloat16)


def weight(here, pieces, first, width, h):
    depth = pieces[2].shape[1]
    rows, inner = h.shape
    in_specs = piece_specs(pieces, first, width)
    in_specs.append(pl.BlockSpec((rows, inner), lambda j, *_: (0, 0)))
    return pl.pallas_call(
        weight_kernel,
        grid_spec=prefetched(
            1,
            (depth // width,),
            in_specs,
            pl.BlockSpec((width, inner), lambda j, *_: (j, 0)),
        ),
        out_shape=jax.ShapeDtypeStruct((depth, inner), jnp.bfloat16),
        compiler_params=room(26),
        cost_estimate=cost(
            2 * rows * depth * inner, 2 * rows * depth + 2 * depth * inner + 2 * rows * inner
        ),
        name="weight",
    )(here, *pieces, h)


def after(x, *others):
    return lax.optimization_barrier((x, *others))[0]


def steps(queries, keys, values, out_gradient, out_weight, segments, counts):
    depth = out_gradient.shape[1]
    half = depth // 2
    here = jnp.stack([lax.axis_index(DP), lax.axis_index("z_lo"), lax.axis_index("core")])
    here = here.astype(jnp.int32)
    ring = [(i, (i + 1) % CHIPS) for i in range(CHIPS)]

    partner = swapped(out_gradient, "core")
    pieces = [[out_gradient, partner] for _ in range(2)]

    def turn(c, x):
        y = lax.ppermute(x, "z_lo", ring)
        z = swapped(y, "core")
        pieces[c] += [y, z]
        return y

    first = turn(0, lax.slice_in_dim(out_gradient, 0, half, axis=1))
    later = lax.slice_in_dim(after(out_gradient, first), half, depth, axis=1)
    second = turn(0, first)
    turn(0, second)
    x = after(later, second)
    for _ in range(3):
        x = turn(1, x)

    chances, head_output, output_turned, keys_turned = forward(here, segments, queries, keys, values)

    partial = project(here, (0, 1, 2, 3), pieces[0], 0, 1280, out_weight, None, None)
    gradient = project(here, (0, 1, 2), pieces[1], half, 1280, out_weight, partial, None)
    gradient = project(here, (3,), pieces[1], half, 1280, out_weight, partial, gradient)

    sums = []
    for c in range(2):
        term = weight(here, pieces[c], c * half, 1280, output_turned)
        tiles = term.reshape(16, -1, term.shape[1])
        tiles = lax.all_to_all(tiles, ("y", "x"), 0, 0, tiled=True)
        sums.append(jnp.sum(tiles.astype(jnp.float32), axis=0))
    upper = lax.axis_index("z_hi") == 1
    kept = jnp.where(upper, sums[1], sums[0])
    sent = jnp.where(upper, sums[0], sums[1]).astype(jnp.bfloat16)
    got = swapped(sent, "z_hi")
    weight_gradient = kept + got.astype(jnp.float32)

    local, arrived = [], []
    shares = ((0, 2), (2, 1))
    for first, heads in shares:
        *local, tail = backward(
            here, segments, first, heads,
            queries, keys_turned, values, gradient, head_output, chances, local,
        )
        arrived.append(swapped(tail, "z_hi"))
    for i, (first, _) in enumerate(shares):
        local = settle(here, counts, first, local, arrived[i])
    return (*local, weight_gradient)


def solution(mesh):
    split = Mesh(mesh.devices.reshape(2, 4, 4, CHIPS, 2), AXES)
    placed = (
        P(DP, TENSOR),
        P(DP, TENSOR),
        P(DP, TENSOR),
        P(AXES, None),
        P(TENSOR, None),
        P(),
        P(),
    )
    return jax.shard_map(
        steps,
        mesh=split,
        in_specs=placed,
        out_specs=(P(DP, TENSOR), P(DP, TENSOR), P(DP, TENSOR), P(DP, TENSOR)),
        check_vma=False,
    )
```

```python
import functools

import jax
import jax.numpy as jnp
from jax import lax
from jax.experimental import pallas as pl
from jax.experimental.pallas import tpu as pltpu
from jax.sharding import Mesh
from jax.sharding import PartitionSpec as P


HEAD_SIZE = 128
BLOCK = 128
WINDOW = 4
MOVABLE = 4
CHIPS = 4
REPLICAS = 32
ROOMY = 58
SCALE = HEAD_SIZE**-0.5
LOG2E = 1.4426950408889634
DP = ("z_hi", "y", "x")
TENSOR = ("z_lo", "core")
AXES = DP + TENSOR

masked_score = -1e30


def swapped(x, axis):
    n = lax.axis_size(axis)
    return lax.ppermute(x, axis, [(i, (i + n // 2) % n) for i in range(n)])


def dot(a, b, over):
    return lax.dot_general(
        a, b, (((over[0],), (over[1],)), ((), ())), preferred_element_type=jnp.float32
    )


def cost(flops, moved, transcendentals=0):
    return pl.CostEstimate(flops=flops, bytes_accessed=moved, transcendentals=transcendentals)


def block_at(index, size=BLOCK):
    return pl.ds(pl.multiple_of(index * size, size), size)


def window_of(ids, row, b):
    blocks = ids.shape[1]
    own = ids[row, b]
    first = jnp.int32(0)
    for j in range(blocks):
        first = first + jnp.where(ids[row, j] < own, 1, 0)
    start = jnp.minimum(first, blocks - WINDOW)
    return own, start, pl.ds(pl.multiple_of(start * BLOCK, BLOCK), WINDOW * BLOCK)


def forward_kernel(here_ref, ids_ref, q_ref, k_ref, v_ref, p_ref, o_ref, r_ref, kt_ref, vt):
    row, chip, core = here_ref[0], here_ref[1], here_ref[2]
    kt_ref[...] = k_ref[...].T
    vt[...] = v_ref[...].T
    for b in range(ids_ref.shape[1]):
        own, start, near = window_of(ids_ref, row, b)
        rows = pl.ds(b * BLOCK, BLOCK)
        scores = dot(k_ref[near, :], q_ref[rows, :], (1, 1))
        tiles = []
        for t in range(WINDOW):
            off = jnp.where(ids_ref[row, start + t] == own, 0.0, masked_score)
            tiles.append(scores[t * BLOCK : (t + 1) * BLOCK] + off)
        top = jnp.max(functools.reduce(jnp.maximum, tiles), axis=0, keepdims=True)
        tiles = [jnp.exp2((x - top) * (SCALE * LOG2E)) for x in tiles]
        total = jnp.sum(functools.reduce(jnp.add, tiles), axis=0, keepdims=True)
        inverse = 1.0 / total
        p = jnp.concatenate([(x * inverse).astype(jnp.bfloat16) for x in tiles], axis=0)
        p_ref[0, b] = p
        o = dot(vt[:, near], p, (1, 0)).T.astype(jnp.bfloat16)
        o_ref[rows, :] = o
        turn = lax.rem(chip + CHIPS - b // 2, CHIPS)
        r_ref[block_at(2 * turn + jnp.where(core == b % 2, 0, 1)), :] = o


def backward_kernel(
    here_ref, ids_ref, q_ref, kt_ref, v_ref, g_ref, o_ref, p_ref, *rest
):
    dq_ref, dk_ref, dv_ref, tail_ref, ka, va = rest[-6:]
    row = here_ref[0]
    front = dq_ref.shape[0] - tail_ref.shape[1]
    ka[...] = jnp.zeros_like(ka)
    va[...] = jnp.zeros_like(va)
    for b in range(ids_ref.shape[1]):
        _, _, near = window_of(ids_ref, row, b)
        rows = pl.ds(b * BLOCK, BLOCK)
        g = g_ref[rows, :]
        p = p_ref[0, b]
        dp = dot(v_ref[near, :], g, (1, 1))
        center = jnp.sum(
            (g.astype(jnp.float32) * o_ref[rows, :].astype(jnp.float32)).T, axis=0, keepdims=True
        )
        ds = (p.astype(jnp.float32) * (dp - center)).astype(jnp.bfloat16)
        dq_ref[rows, :] = (dot(kt_ref[:, near], ds, (1, 0)) * SCALE).T.astype(jnp.bfloat16)
        ka[near, :] += dot(ds, q_ref[rows, :], (1, 0))
        va[near, :] += dot(p, g, (1, 0))
    dk_ref[...] = (ka[...] * SCALE).astype(jnp.bfloat16)
    dv_ref[...] = va[...].astype(jnp.bfloat16)
    for i, ref in enumerate((dq_ref, dk_ref, dv_ref)):
        tail_ref[i] = ref[front:, :]


def settle_kernel(column, here_ref, counts_ref, *refs):
    arrived_ref, outs, sems = refs[3], refs[4:7], refs[7]
    moving = counts_ref[here_ref[0]]
    front = outs[0].shape[0] - arrived_ref.shape[1]

    def copy(i, b):
        return pltpu.make_async_copy(
            arrived_ref.at[i, pl.ds(b * BLOCK, BLOCK), :],
            outs[i].at[pl.ds(front + b * BLOCK, BLOCK), pl.ds(column, arrived_ref.shape[2])],
            sems.at[i, b],
        )

    for b in range(MOVABLE):

        @pl.when(b >= MOVABLE - moving)
        def _():
            for i in range(3):
                copy(i, b).start()

    for b in range(MOVABLE):

        @pl.when(b >= MOVABLE - moving)
        def _():
            for i in range(3):
                copy(i, b).wait()


def room(mebibytes):
    return pltpu.CompilerParams(vmem_limit_bytes=mebibytes * 2**20)


def prefetched(scalars, grid, in_specs, out_specs, scratch_shapes=()):
    return pltpu.PrefetchScalarGridSpec(
        num_scalar_prefetch=scalars,
        grid=grid,
        in_specs=in_specs,
        out_specs=out_specs,
        scratch_shapes=scratch_shapes,
    )


ANY = pl.BlockSpec(memory_space=pl.ANY)


def forward(here, ids, q, k, v):
    rows, inner = q.shape
    heads, blocks = inner // HEAD_SIZE, rows // BLOCK
    keys = WINDOW * BLOCK
    hs = pl.BlockSpec((rows, HEAD_SIZE), lambda h, *_: (0, h))
    ps = pl.BlockSpec((1, blocks, keys, BLOCK), lambda h, *_: (h, 0, 0, 0))
    ts = pl.BlockSpec((HEAD_SIZE, rows), lambda h, *_: (h, 0))
    out = jax.ShapeDtypeStruct((rows, inner), jnp.bfloat16)
    return pl.pallas_call(
        forward_kernel,
        grid_spec=prefetched(
            2,
            (heads,),
            [hs] * 3,
            [ps, hs, hs, ts],
            [pltpu.VMEM((HEAD_SIZE, rows), jnp.bfloat16)],
        ),
        out_shape=[
            jax.ShapeDtypeStruct((heads, blocks, keys, BLOCK), jnp.bfloat16),
            out,
            out,
            jax.ShapeDtypeStruct((inner, rows), jnp.bfloat16),
        ],
        compiler_params=room(ROOMY),
        cost_estimate=cost(
            4 * rows * keys * inner,
            12 * rows * inner + 2 * heads * rows * keys,
            heads * rows * keys,
        ),
        name="forward",
    )(here, ids, *map(in_hbm, (q, k, v)))


def backward(here, ids, first, heads, q, kt, v, g, o, p, before):
    rows, inner = q.shape
    blocks = rows // BLOCK
    keys = WINDOW * BLOCK
    moving = MOVABLE * BLOCK
    hs = pl.BlockSpec((rows, HEAD_SIZE), lambda h, *_: (0, first + h))
    ps = pl.BlockSpec((1, blocks, keys, BLOCK), lambda h, *_: (first + h, 0, 0, 0))
    ts = pl.BlockSpec((HEAD_SIZE, rows), lambda h, *_: (first + h, 0))
    return pl.pallas_call(
        backward_kernel,
        grid_spec=prefetched(
            2,
            (heads,),
            [hs, ts, hs, hs, hs, ps] + [ANY] * len(before),
            [hs] * 3 + [pl.BlockSpec((3, moving, HEAD_SIZE), lambda h, *_: (0, 0, h))],
            [pltpu.VMEM((rows, HEAD_SIZE), jnp.float32)] * 2,
        ),
        out_shape=[jax.ShapeDtypeStruct((rows, inner), jnp.bfloat16)] * 3
        + [jax.ShapeDtypeStruct((3, moving, heads * HEAD_SIZE), jnp.bfloat16)],
        input_output_aliases={8 + i: i for i in range(len(before))},
        compiler_params=room(ROOMY),
        cost_estimate=cost(
            8 * rows * keys * heads * HEAD_SIZE,
            19 * rows * heads * HEAD_SIZE + 2 * heads * rows * keys,
        ),
        name="backward",
    )(here, ids, *map(in_hbm, (q, kt, v, g, o, p)), *before)


def settle(here, counts, first, local, arrived):
    return pl.pallas_call(
        functools.partial(settle_kernel, first * HEAD_SIZE),
        grid_spec=prefetched(
            2,
            (1,),
            [ANY] * 3 + [pl.BlockSpec(memory_space=pltpu.VMEM)],
            [ANY] * 3,
            [pltpu.SemaphoreType.DMA((3, MOVABLE))],
        ),
        out_shape=[jax.ShapeDtypeStruct(x.shape, x.dtype) for x in local],
        input_output_aliases={2 + i: i for i in range(3)},
        compiler_params=room(8),
        cost_estimate=cost(0, 4 * arrived.size),
        name="settle",
    )(here, counts, *local, arrived)


def project_kernel(turns, final, here_ref, *refs):
    count = 2 * len(turns)
    pieces, w_ref = refs[:count], refs[count]
    out_ref, acc = refs[-2:]
    step = pl.program_id(0)
    part = dot(jnp.concatenate([ref[...] for ref in pieces], axis=0), w_ref[...], (1, 1))

    @pl.when(step == 0)
    def _():
        acc[...] = refs[count + 1][...] + part if final else part

    @pl.when(step > 0)
    def _():
        acc[...] += part

    @pl.when(step == pl.num_programs(0) - 1)
    def _():
        if not final:
            out_ref[...] = acc[...]
            return
        chip, core = here_ref[1], here_ref[2]
        for i in range(count):
            block = core if i % 2 == 0 else 1 - core
            if len(turns) > 1:
                block += 2 * lax.rem(chip + CHIPS - turns[i // 2], CHIPS)
            out_ref[block_at(block), :] = acc[i * BLOCK : (i + 1) * BLOCK].astype(jnp.bfloat16)


def piece_specs(pieces, first, width):
    def spec(x):
        at = first // width if x.shape[1] > pieces[-1].shape[1] else 0
        return pl.BlockSpec((x.shape[0], width), lambda j, *_: (0, at + j))

    return [spec(x) for x in pieces]


def in_hbm(x):
    return pltpu.with_memory_space_constraint(x, pltpu.HBM)


def project(here, turns, pieces, first, width, w, partial, before):
    pieces = [x for t in turns for x in pieces[2 * t : 2 * t + 2]]
    depth = pieces[-1].shape[1]
    rows = sum(x.shape[0] for x in pieces)
    inner = w.shape[0]
    at, place = first // width, turns[0] * 2 * BLOCK // rows
    final = partial is not None
    in_specs = piece_specs(pieces, first, width)
    in_specs.append(pl.BlockSpec((inner, width), lambda j, *_: (0, at + j)))
    operands = [*map(in_hbm, pieces), in_hbm(w)]
    aliases = {}
    total = rows
    out_spec = pl.BlockSpec((rows, inner), lambda j, *_: (0, 0))
    if final:
        total = partial.shape[0]
        in_specs.append(pl.BlockSpec((rows, inner), lambda j, *_: (place, 0)))
        operands.append(in_hbm(partial))
        out_spec = pl.BlockSpec((total, inner), lambda j, *_: (0, 0))
    if before is not None:
        in_specs.append(ANY)
        operands.append(before)
        aliases = {len(operands): 0}
        out_spec = pl.BlockSpec(
            (rows, inner), lambda j, here: (lax.rem(here[1] + CHIPS - turns[0], CHIPS), 0)
        )
    return pl.pallas_call(
        functools.partial(project_kernel, turns, final),
        grid_spec=prefetched(
            1, (depth // width,), in_specs, out_spec, [pltpu.VMEM((rows, inner), jnp.float32)]
        ),
        out_shape=jax.ShapeDtypeStruct((total, inner), jnp.bfloat16 if final else jnp.float32),
        input_output_aliases=aliases,
        compiler_params=room(ROOMY),
        cost_estimate=cost(
            2 * rows * depth * inner, 2 * rows * depth + 2 * inner * depth + 8 * rows * inner
        ),
        name="project",
    )(here, *operands)


def weight_kernel(here_ref, *refs):
    pieces, h_ref, out_ref = refs[: 2 * CHIPS], refs[2 * CHIPS], refs[-1]
    g = jnp.concatenate([ref[...] for ref in pieces], axis=0)
    out_ref[...] = (dot(g, h_ref[...], (0, 0)) * (1.0 / REPLICAS)).astype(jnp.bfloat16)


def weight(here, pieces, first, width, h):
    depth = pieces[2].shape[1]
    rows, inner = h.shape
    in_specs = piece_specs(pieces, first, width)
    in_specs.append(pl.BlockSpec((rows, inner), lambda j, *_: (0, 0)))
    return pl.pallas_call(
        weight_kernel,
        grid_spec=prefetched(
            1,
            (depth // width,),
            in_specs,
            pl.BlockSpec((width, inner), lambda j, *_: (j, 0)),
        ),
        out_shape=jax.ShapeDtypeStruct((depth, inner), jnp.bfloat16),
        compiler_params=room(ROOMY),
        cost_estimate=cost(
            2 * rows * depth * inner, 2 * rows * depth + 2 * depth * inner + 2 * rows * inner
        ),
        name="weight",
    )(here, *map(in_hbm, pieces), h)


def after(x, *others):
    return lax.optimization_barrier((x, *others))[0]


def steps(queries, keys, values, out_gradient, out_weight, segments, counts):
    depth = out_gradient.shape[1]
    half = depth // 2
    here = jnp.stack([lax.axis_index(DP), lax.axis_index("z_lo"), lax.axis_index("core")])
    here = here.astype(jnp.int32)
    ring = [(i, (i + 1) % CHIPS) for i in range(CHIPS)]

    partner = swapped(out_gradient, "core")
    pieces = [[out_gradient, partner] for _ in range(2)]

    def turn(c, x):
        y = lax.ppermute(x, "z_lo", ring)
        z = swapped(y, "core")
        pieces[c] += [y, z]
        return y

    first = turn(0, lax.slice_in_dim(out_gradient, 0, half, axis=1))
    later = lax.slice_in_dim(after(out_gradient, first), half, depth, axis=1)
    second = turn(0, first)
    turn(0, second)
    x = after(later, second)
    for _ in range(3):
        x = turn(1, x)

    chances, head_output, output_turned, keys_turned = forward(here, segments, queries, keys, values)

    partial = project(here, (0, 1, 2, 3), pieces[0], 0, 1280, out_weight, None, None)
    gradient = project(here, (0, 1, 2), pieces[1], half, 1280, out_weight, partial, None)
    gradient = project(here, (3,), pieces[1], half, 1280, out_weight, partial, gradient)

    sums = []
    for c in range(2):
        term = weight(here, pieces[c], c * half, 1280, output_turned)
        tiles = term.reshape(16, -1, term.shape[1])
        tiles = lax.all_to_all(tiles, ("y", "x"), 0, 0, tiled=True)
        sums.append(jnp.sum(tiles.astype(jnp.float32), axis=0))
    upper = lax.axis_index("z_hi") == 1
    kept = jnp.where(upper, sums[1], sums[0])
    sent = jnp.where(upper, sums[0], sums[1]).astype(jnp.bfloat16)
    got = swapped(sent, "z_hi")
    weight_gradient = kept + got.astype(jnp.float32)

    local, arrived = [], []
    shares = ((0, 2), (2, 1))
    for first, heads in shares:
        *local, tail = backward(
            here, segments, first, heads,
            queries, keys_turned, values, gradient, head_output, chances, local,
        )
        arrived.append(swapped(tail, "z_hi"))
    for i, (first, _) in enumerate(shares):
        local = settle(here, counts, first, local, arrived[i])
    return (*local, weight_gradient)


def solution(mesh):
    split = Mesh(mesh.devices.reshape(2, 4, 4, CHIPS, 2), AXES)
    placed = (
        P(DP, TENSOR),
        P(DP, TENSOR),
        P(DP, TENSOR),
        P(AXES, None),
        P(TENSOR, None),
        P(),
        P(),
    )
    return jax.shard_map(
        steps,
        mesh=split,
        in_specs=placed,
        out_specs=(P(DP, TENSOR), P(DP, TENSOR), P(DP, TENSOR), P(DP, TENSOR)),
        check_vma=False,
    )
```

```python
import functools

import jax
import jax.numpy as jnp
from jax import lax
from jax.experimental import pallas as pl
from jax.experimental.pallas import tpu as pltpu
from jax.sharding import Mesh
from jax.sharding import PartitionSpec as P


HEAD_SIZE = 128
BLOCK = 128
WINDOW = 4
MOVABLE = 4
CHIPS = 4
REPLICAS = 32
SCALE = HEAD_SIZE**-0.5
LOG2E = 1.4426950408889634
DP = ("z_hi", "y", "x")
TENSOR = ("z_lo", "core")
AXES = DP + TENSOR

masked_score = -1e30


def swapped(x, axis):
    n = lax.axis_size(axis)
    return lax.ppermute(x, axis, [(i, (i + n // 2) % n) for i in range(n)])


def dot(a, b, over):
    return lax.dot_general(
        a, b, (((over[0],), (over[1],)), ((), ())), preferred_element_type=jnp.float32
    )


def cost(flops, moved, transcendentals=0):
    return pl.CostEstimate(flops=flops, bytes_accessed=moved, transcendentals=transcendentals)


def block_at(index, size=BLOCK):
    return pl.ds(pl.multiple_of(index * size, size), size)


def window_of(ids, row, b):
    blocks = ids.shape[1]
    own = ids[row, b]
    first = jnp.int32(0)
    for j in range(blocks):
        first = first + jnp.where(ids[row, j] < own, 1, 0)
    start = jnp.minimum(first, blocks - WINDOW)
    return own, start, pl.ds(pl.multiple_of(start * BLOCK, BLOCK), WINDOW * BLOCK)


def forward_kernel(here_ref, ids_ref, q_ref, k_ref, v_ref, p_ref, o_ref, r_ref, kt_ref, vt):
    row, chip, core = here_ref[0], here_ref[1], here_ref[2]
    kt_ref[...] = k_ref[...].T
    vt[...] = v_ref[...].T
    for b in range(ids_ref.shape[1]):
        own, start, near = window_of(ids_ref, row, b)
        rows = pl.ds(b * BLOCK, BLOCK)
        scores = dot(k_ref[near, :], q_ref[rows, :], (1, 1))
        tiles = []
        for t in range(WINDOW):
            off = jnp.where(ids_ref[row, start + t] == own, 0.0, masked_score)
            tiles.append(scores[t * BLOCK : (t + 1) * BLOCK] + off)
        top = jnp.max(functools.reduce(jnp.maximum, tiles), axis=0, keepdims=True)
        tiles = [jnp.exp2((x - top) * (SCALE * LOG2E)) for x in tiles]
        total = jnp.sum(functools.reduce(jnp.add, tiles), axis=0, keepdims=True)
        inverse = 1.0 / total
        p = jnp.concatenate([(x * inverse).astype(jnp.bfloat16) for x in tiles], axis=0)
        p_ref[0, b] = p
        o = dot(vt[:, near], p, (1, 0)).T.astype(jnp.bfloat16)
        o_ref[rows, :] = o
        turn = lax.rem(chip + CHIPS - b // 2, CHIPS)
        r_ref[block_at(2 * turn + jnp.where(core == b % 2, 0, 1)), :] = o


def backward_kernel(
    here_ref, ids_ref, q_ref, kt_ref, v_ref, g_ref, o_ref, p_ref, *rest
):
    dq_ref, dk_ref, dv_ref, tail_ref, both = rest[-5:]
    row = here_ref[0]
    front = dq_ref.shape[0] - tail_ref.shape[1]
    both[...] = jnp.zeros_like(both)
    none = jnp.zeros((BLOCK, HEAD_SIZE), jnp.bfloat16)
    for b in range(ids_ref.shape[1]):
        _, _, near = window_of(ids_ref, row, b)
        rows = pl.ds(b * BLOCK, BLOCK)
        g = g_ref[rows, :]
        p = p_ref[0, b]
        dp = dot(v_ref[near, :], g, (1, 1))
        center = jnp.sum(
            (g.astype(jnp.float32) * o_ref[rows, :].astype(jnp.float32)).T, axis=0, keepdims=True
        )
        ds = (p.astype(jnp.float32) * (dp - center)).astype(jnp.bfloat16)
        dq_ref[rows, :] = (dot(kt_ref[:, near], ds, (1, 0)) * SCALE).T.astype(jnp.bfloat16)
        pair = jnp.concatenate(
            [
                jnp.concatenate([q_ref[rows, :], none], axis=1),
                jnp.concatenate([none, g], axis=1),
            ],
            axis=0,
        )
        both[near, :] += dot(jnp.concatenate([ds, p], axis=1), pair, (1, 0))
    dk_ref[...] = (both[:, :HEAD_SIZE] * SCALE).astype(jnp.bfloat16)
    dv_ref[...] = both[:, HEAD_SIZE:].astype(jnp.bfloat16)
    for i, ref in enumerate((dq_ref, dk_ref, dv_ref)):
        tail_ref[i] = ref[front:, :]


def settle_kernel(column, here_ref, counts_ref, *refs):
    arrived_ref, outs, sems = refs[3], refs[4:7], refs[7]
    moving = counts_ref[here_ref[0]]
    front = outs[0].shape[0] - arrived_ref.shape[1]

    def copy(i, b):
        return pltpu.make_async_copy(
            arrived_ref.at[i, pl.ds(b * BLOCK, BLOCK), :],
            outs[i].at[pl.ds(front + b * BLOCK, BLOCK), pl.ds(column, arrived_ref.shape[2])],
            sems.at[i, b],
        )

    for b in range(MOVABLE):

        @pl.when(b >= MOVABLE - moving)
        def _():
            for i in range(3):
                copy(i, b).start()

    for b in range(MOVABLE):

        @pl.when(b >= MOVABLE - moving)
        def _():
            for i in range(3):
                copy(i, b).wait()


def room(mebibytes):
    return pltpu.CompilerParams(vmem_limit_bytes=mebibytes * 2**20)


def prefetched(scalars, grid, in_specs, out_specs, scratch_shapes=()):
    return pltpu.PrefetchScalarGridSpec(
        num_scalar_prefetch=scalars,
        grid=grid,
        in_specs=in_specs,
        out_specs=out_specs,
        scratch_shapes=scratch_shapes,
    )


ANY = pl.BlockSpec(memory_space=pl.ANY)


def forward(here, ids, q, k, v):
    rows, inner = q.shape
    heads, blocks = inner // HEAD_SIZE, rows // BLOCK
    keys = WINDOW * BLOCK
    hs = pl.BlockSpec((rows, HEAD_SIZE), lambda h, *_: (0, h))
    ps = pl.BlockSpec((1, blocks, keys, BLOCK), lambda h, *_: (h, 0, 0, 0))
    ts = pl.BlockSpec((HEAD_SIZE, rows), lambda h, *_: (h, 0))
    out = jax.ShapeDtypeStruct((rows, inner), jnp.bfloat16)
    return pl.pallas_call(
        forward_kernel,
        grid_spec=prefetched(
            2,
            (heads,),
            [hs] * 3,
            [ps, hs, hs, ts],
            [pltpu.VMEM((HEAD_SIZE, rows), jnp.bfloat16)],
        ),
        out_shape=[
            jax.ShapeDtypeStruct((heads, blocks, keys, BLOCK), jnp.bfloat16),
            out,
            out,
            jax.ShapeDtypeStruct((inner, rows), jnp.bfloat16),
        ],
        compiler_params=room(20),
        cost_estimate=cost(
            4 * rows * keys * inner,
            12 * rows * inner + 2 * heads * rows * keys,
            heads * rows * keys,
        ),
        name="forward",
    )(here, ids, q, k, v)


def backward(here, ids, first, heads, q, kt, v, g, o, p, before):
    rows, inner = q.shape
    blocks = rows // BLOCK
    keys = WINDOW * BLOCK
    moving = MOVABLE * BLOCK
    hs = pl.BlockSpec((rows, HEAD_SIZE), lambda h, *_: (0, first + h))
    ps = pl.BlockSpec((1, blocks, keys, BLOCK), lambda h, *_: (first + h, 0, 0, 0))
    ts = pl.BlockSpec((HEAD_SIZE, rows), lambda h, *_: (first + h, 0))
    return pl.pallas_call(
        backward_kernel,
        grid_spec=prefetched(
            2,
            (heads,),
            [hs, ts, hs, hs, hs, ps] + [ANY] * len(before),
            [hs] * 3 + [pl.BlockSpec((3, moving, HEAD_SIZE), lambda h, *_: (0, 0, h))],
            [pltpu.VMEM((rows, 2 * HEAD_SIZE), jnp.float32)],
        ),
        out_shape=[jax.ShapeDtypeStruct((rows, inner), jnp.bfloat16)] * 3
        + [jax.ShapeDtypeStruct((3, moving, heads * HEAD_SIZE), jnp.bfloat16)],
        input_output_aliases={8 + i: i for i in range(len(before))},
        compiler_params=room(20),
        cost_estimate=cost(
            8 * rows * keys * heads * HEAD_SIZE,
            19 * rows * heads * HEAD_SIZE + 2 * heads * rows * keys,
        ),
        name="backward",
    )(here, ids, q, kt, v, g, o, p, *before)


def settle(here, counts, first, local, arrived):
    return pl.pallas_call(
        functools.partial(settle_kernel, first * HEAD_SIZE),
        grid_spec=prefetched(
            2,
            (1,),
            [ANY] * 3 + [pl.BlockSpec(memory_space=pltpu.VMEM)],
            [ANY] * 3,
            [pltpu.SemaphoreType.DMA((3, MOVABLE))],
        ),
        out_shape=[jax.ShapeDtypeStruct(x.shape, x.dtype) for x in local],
        input_output_aliases={2 + i: i for i in range(3)},
        compiler_params=room(8),
        cost_estimate=cost(0, 4 * arrived.size),
        name="settle",
    )(here, counts, *local, arrived)


def project_kernel(turns, final, here_ref, *refs):
    count = 2 * len(turns)
    pieces, w_ref = refs[:count], refs[count]
    out_ref, acc = refs[-2:]
    step = pl.program_id(0)
    part = dot(jnp.concatenate([ref[...] for ref in pieces], axis=0), w_ref[...], (1, 1))

    @pl.when(step == 0)
    def _():
        acc[...] = refs[count + 1][...] + part if final else part

    @pl.when(step > 0)
    def _():
        acc[...] += part

    @pl.when(step == pl.num_programs(0) - 1)
    def _():
        if not final:
            out_ref[...] = acc[...]
            return
        chip, core = here_ref[1], here_ref[2]
        for i in range(count):
            block = core if i % 2 == 0 else 1 - core
            if len(turns) > 1:
                block += 2 * lax.rem(chip + CHIPS - turns[i // 2], CHIPS)
            out_ref[block_at(block), :] = acc[i * BLOCK : (i + 1) * BLOCK].astype(jnp.bfloat16)


def piece_specs(pieces, first, width):
    def spec(x):
        at = first // width if x.shape[1] > pieces[-1].shape[1] else 0
        return pl.BlockSpec((x.shape[0], width), lambda j, *_: (0, at + j))

    return [spec(x) for x in pieces]


def in_hbm(x):
    return pltpu.with_memory_space_constraint(x, pltpu.HBM)


def project(here, turns, pieces, first, width, w, partial, before):
    pieces = [x for t in turns for x in pieces[2 * t : 2 * t + 2]]
    depth = pieces[-1].shape[1]
    rows = sum(x.shape[0] for x in pieces)
    inner = w.shape[0]
    at, place = first // width, turns[0] * 2 * BLOCK // rows
    final = partial is not None
    in_specs = piece_specs(pieces, first, width)
    in_specs.append(pl.BlockSpec((inner, width), lambda j, *_: (0, at + j)))
    operands = [*pieces, in_hbm(w)]
    aliases = {}
    total = rows
    out_spec = pl.BlockSpec((rows, inner), lambda j, *_: (0, 0))
    if final:
        total = partial.shape[0]
        in_specs.append(pl.BlockSpec((rows, inner), lambda j, *_: (place, 0)))
        operands.append(partial)
        out_spec = pl.BlockSpec((total, inner), lambda j, *_: (0, 0))
    if before is not None:
        in_specs.append(ANY)
        operands.append(before)
        aliases = {len(operands): 0}
        out_spec = pl.BlockSpec(
            (rows, inner), lambda j, here: (lax.rem(here[1] + CHIPS - turns[0], CHIPS), 0)
        )
    return pl.pallas_call(
        functools.partial(project_kernel, turns, final),
        grid_spec=prefetched(
            1, (depth // width,), in_specs, out_spec, [pltpu.VMEM((rows, inner), jnp.float32)]
        ),
        out_shape=jax.ShapeDtypeStruct((total, inner), jnp.bfloat16)
        if final
        else pltpu.HBM((total, inner), jnp.float32),
        input_output_aliases=aliases,
        compiler_params=room(30),
        cost_estimate=cost(
            2 * rows * depth * inner, 2 * rows * depth + 2 * inner * depth + 8 * rows * inner
        ),
        name="project",
    )(here, *operands)


def weight_kernel(here_ref, *refs):
    pieces, h_ref, out_ref = refs[: 2 * CHIPS], refs[2 * CHIPS], refs[-1]
    g = jnp.concatenate([ref[...] for ref in pieces], axis=0)
    term = (dot(g, h_ref[...], (0, 0)) * (1.0 / REPLICAS)).astype(jnp.bfloat16)
    out_ref[...] = term.reshape(out_ref.shape)


def weight(here, pieces, first, width, h):
    depth = pieces[2].shape[1]
    rows, inner = h.shape
    in_specs = piece_specs(pieces, first, width)
    in_specs.append(pl.BlockSpec((rows, inner), lambda j, *_: (0, 0)))
    return pl.pallas_call(
        weight_kernel,
        grid_spec=prefetched(
            1,
            (depth // width,),
            in_specs,
            pl.BlockSpec((16 * width // depth, depth // 16, inner), lambda j, *_: (j, 0, 0)),
        ),
        out_shape=pltpu.HBM((16, depth // 16, inner), jnp.bfloat16),
        compiler_params=room(26),
        cost_estimate=cost(
            2 * rows * depth * inner, 2 * rows * depth + 2 * depth * inner + 2 * rows * inner
        ),
        name="weight",
    )(here, *pieces, h)


def after(x, *others):
    return lax.optimization_barrier((x, *others))[0]


def steps(queries, keys, values, out_gradient, out_weight, segments, counts):
    depth = out_gradient.shape[1]
    half = depth // 2
    here = jnp.stack([lax.axis_index(DP), lax.axis_index("z_lo"), lax.axis_index("core")])
    here = here.astype(jnp.int32)
    ring = [(i, (i + 1) % CHIPS) for i in range(CHIPS)]

    partner = swapped(out_gradient, "core")
    pieces = [[out_gradient, partner] for _ in range(2)]

    def turn(c, x):
        y = lax.ppermute(x, "z_lo", ring)
        z = swapped(y, "core")
        pieces[c] += [y, z]
        return y

    first = turn(0, lax.slice_in_dim(out_gradient, 0, half, axis=1))
    later = lax.slice_in_dim(after(out_gradient, first), half, depth, axis=1)
    second = turn(0, first)
    turn(0, second)
    x = after(later, second)
    for _ in range(3):
        x = turn(1, x)

    chances, head_output, output_turned, keys_turned = forward(here, segments, queries, keys, values)

    partial = project(here, (0, 1, 2, 3), pieces[0], 0, 1280, out_weight, None, None)
    gradient = project(here, (0, 1, 2), pieces[1], half, 1280, out_weight, partial, None)
    gradient = project(here, (3,), pieces[1], half, 1280, out_weight, partial, gradient)

    sums = []
    for c in range(2):
        tiles = weight(here, pieces[c], c * half, 1280, output_turned)
        tiles = lax.all_to_all(tiles, ("y", "x"), 0, 0, tiled=True)
        sums.append(jnp.sum(tiles.astype(jnp.float32), axis=0))
    upper = lax.axis_index("z_hi") == 1
    kept = jnp.where(upper, sums[1], sums[0])
    sent = jnp.where(upper, sums[0], sums[1]).astype(jnp.bfloat16)
    got = swapped(sent, "z_hi")
    weight_gradient = kept + got.astype(jnp.float32)

    local, arrived = [], []
    shares = ((0, 2), (2, 1))
    for first, heads in shares:
        *local, tail = backward(
            here, segments, first, heads,
            queries, keys_turned, values, gradient, head_output, chances, local,
        )
        arrived.append(swapped(tail, "z_hi"))
    for i, (first, _) in enumerate(shares):
        local = settle(here, counts, first, local, arrived[i])
    return (*local, weight_gradient)


def solution(mesh):
    split = Mesh(mesh.devices.reshape(2, 4, 4, CHIPS, 2), AXES)
    placed = (
        P(DP, TENSOR),
        P(DP, TENSOR),
        P(DP, TENSOR),
        P(AXES, None),
        P(TENSOR, None),
        P(),
        P(),
    )
    return jax.shard_map(
        steps,
        mesh=split,
        in_specs=placed,
        out_specs=(P(DP, TENSOR), P(DP, TENSOR), P(DP, TENSOR), P(DP, TENSOR)),
        check_vma=False,
    )
```

```python
import functools

import jax
import jax.numpy as jnp
from jax import lax
from jax.experimental import pallas as pl
from jax.experimental.pallas import tpu as pltpu
from jax.sharding import Mesh
from jax.sharding import PartitionSpec as P


HEAD_SIZE = 128
BLOCK = 128
WINDOW = 4
MOVABLE = 4
CHIPS = 4
REPLICAS = 32
SCALE = HEAD_SIZE**-0.5
LOG2E = 1.4426950408889634
DP = ("z_hi", "y", "x")
TENSOR = ("z_lo", "core")
AXES = DP + TENSOR

masked_score = -1e30


def swapped(x, axis):
    n = lax.axis_size(axis)
    return lax.ppermute(x, axis, [(i, (i + n // 2) % n) for i in range(n)])


def dot(a, b, over):
    return lax.dot_general(
        a, b, (((over[0],), (over[1],)), ((), ())), preferred_element_type=jnp.float32
    )


def cost(flops, moved, transcendentals=0):
    return pl.CostEstimate(flops=flops, bytes_accessed=moved, transcendentals=transcendentals)


def block_at(index, size=BLOCK):
    return pl.ds(pl.multiple_of(index * size, size), size)


def window_of(ids, row, b):
    blocks = ids.shape[1]
    own = ids[row, b]
    first = jnp.int32(0)
    for j in range(blocks):
        first = first + jnp.where(ids[row, j] < own, 1, 0)
    start = jnp.minimum(first, blocks - WINDOW)
    return own, start, pl.ds(pl.multiple_of(start * BLOCK, BLOCK), WINDOW * BLOCK)


def forward_kernel(here_ref, ids_ref, q_ref, k_ref, v_ref, p_ref, o_ref, r_ref, kt_ref, vt):
    row, chip, core = here_ref[0], here_ref[1], here_ref[2]
    kt_ref[...] = k_ref[...].T
    vt[...] = v_ref[...].T
    for b in range(ids_ref.shape[1]):
        own, start, near = window_of(ids_ref, row, b)
        rows = pl.ds(b * BLOCK, BLOCK)
        scores = dot(k_ref[near, :], q_ref[rows, :], (1, 1))
        tiles = []
        for t in range(WINDOW):
            off = jnp.where(ids_ref[row, start + t] == own, 0.0, masked_score)
            tiles.append(scores[t * BLOCK : (t + 1) * BLOCK] + off)
        top = jnp.max(functools.reduce(jnp.maximum, tiles), axis=0, keepdims=True)
        tiles = [jnp.exp2((x - top) * (SCALE * LOG2E)) for x in tiles]
        total = jnp.sum(functools.reduce(jnp.add, tiles), axis=0, keepdims=True)
        inverse = 1.0 / total
        p = jnp.concatenate([(x * inverse).astype(jnp.bfloat16) for x in tiles], axis=0)
        p_ref[0, b] = p
        o = dot(vt[:, near], p, (1, 0)).T.astype(jnp.bfloat16)
        o_ref[rows, :] = o
        turn = lax.rem(chip + CHIPS - b // 2, CHIPS)
        r_ref[block_at(2 * turn + jnp.where(core == b % 2, 0, 1)), :] = o


def backward_kernel(
    tail_only, here_ref, ids_ref, q_ref, kt_ref, v_ref, g_ref, o_ref, p_ref, *rest
):
    tail_ref, ka, va = rest[-3:]
    row = here_ref[0]
    blocks = ids_ref.shape[1]
    front = (blocks - MOVABLE) * BLOCK
    ka[...] = jnp.zeros_like(ka)
    va[...] = jnp.zeros_like(va)
    for b in range(blocks - MOVABLE if tail_only else 0, blocks):
        _, _, near = window_of(ids_ref, row, b)
        rows = pl.ds(b * BLOCK, BLOCK)
        g = g_ref[rows, :]
        p = p_ref[0, b]
        dp = dot(v_ref[near, :], g, (1, 1))
        center = jnp.sum(
            (g.astype(jnp.float32) * o_ref[rows, :].astype(jnp.float32)).T, axis=0, keepdims=True
        )
        ds = (p.astype(jnp.float32) * (dp - center)).astype(jnp.bfloat16)
        dq = (dot(kt_ref[:, near], ds, (1, 0)) * SCALE).T.astype(jnp.bfloat16)
        if not tail_only:
            rest[0][rows, :] = dq
        if b * BLOCK >= front:
            tail_ref[0, pl.ds(b * BLOCK - front, BLOCK), :] = dq
        ka[near, :] += dot(ds, q_ref[rows, :], (1, 0))
        va[near, :] += dot(p, g, (1, 0))
    tail_ref[1] = (ka[front:] * SCALE).astype(jnp.bfloat16)
    tail_ref[2] = va[front:].astype(jnp.bfloat16)
    if not tail_only:
        rest[1][...] = (ka[...] * SCALE).astype(jnp.bfloat16)
        rest[2][...] = va[...].astype(jnp.bfloat16)


def settle_kernel(column, here_ref, counts_ref, *refs):
    arrived_ref, outs, sems = refs[3], refs[4:7], refs[7]
    moving = counts_ref[here_ref[0]]
    front = outs[0].shape[0] - arrived_ref.shape[1]

    def copy(i, b):
        return pltpu.make_async_copy(
            arrived_ref.at[i, pl.ds(b * BLOCK, BLOCK), :],
            outs[i].at[pl.ds(front + b * BLOCK, BLOCK), pl.ds(column, arrived_ref.shape[2])],
            sems.at[i, b],
        )

    for b in range(MOVABLE):

        @pl.when(b >= MOVABLE - moving)
        def _():
            for i in range(3):
                copy(i, b).start()

    for b in range(MOVABLE):

        @pl.when(b >= MOVABLE - moving)
        def _():
            for i in range(3):
                copy(i, b).wait()


def room(mebibytes):
    return pltpu.CompilerParams(vmem_limit_bytes=mebibytes * 2**20)


def prefetched(scalars, grid, in_specs, out_specs, scratch_shapes=()):
    return pltpu.PrefetchScalarGridSpec(
        num_scalar_prefetch=scalars,
        grid=grid,
        in_specs=in_specs,
        out_specs=out_specs,
        scratch_shapes=scratch_shapes,
    )


ANY = pl.BlockSpec(memory_space=pl.ANY)


def forward(here, ids, q, k, v):
    rows, inner = q.shape
    heads, blocks = inner // HEAD_SIZE, rows // BLOCK
    keys = WINDOW * BLOCK
    hs = pl.BlockSpec((rows, HEAD_SIZE), lambda h, *_: (0, h))
    ps = pl.BlockSpec((1, blocks, keys, BLOCK), lambda h, *_: (h, 0, 0, 0))
    ts = pl.BlockSpec((HEAD_SIZE, rows), lambda h, *_: (h, 0))
    out = jax.ShapeDtypeStruct((rows, inner), jnp.bfloat16)
    return pl.pallas_call(
        forward_kernel,
        grid_spec=prefetched(
            2,
            (heads,),
            [hs] * 3,
            [ps, hs, hs, ts],
            [pltpu.VMEM((HEAD_SIZE, rows), jnp.bfloat16)],
        ),
        out_shape=[
            jax.ShapeDtypeStruct((heads, blocks, keys, BLOCK), jnp.bfloat16),
            out,
            out,
            jax.ShapeDtypeStruct((inner, rows), jnp.bfloat16),
        ],
        compiler_params=room(20),
        cost_estimate=cost(
            4 * rows * keys * inner,
            12 * rows * inner + 2 * heads * rows * keys,
            heads * rows * keys,
        ),
        name="forward",
    )(here, ids, q, k, v)


def backward(here, ids, heads, tail_only, q, kt, v, g, o, p):
    rows, inner = q.shape
    blocks = rows // BLOCK
    keys = WINDOW * BLOCK
    moving = MOVABLE * BLOCK
    hs = pl.BlockSpec((rows, HEAD_SIZE), lambda h, *_: (0, h))
    ps = pl.BlockSpec((1, blocks, keys, BLOCK), lambda h, *_: (h, 0, 0, 0))
    ts = pl.BlockSpec((HEAD_SIZE, rows), lambda h, *_: (h, 0))
    tails = heads if tail_only else 1
    tail = pl.BlockSpec((3, moving, HEAD_SIZE), lambda h, *_: (0, 0, h if tail_only else 0))
    out = jax.ShapeDtypeStruct((rows, inner), jnp.bfloat16)
    whole = 0 if tail_only else 3
    return pl.pallas_call(
        functools.partial(backward_kernel, tail_only),
        grid_spec=prefetched(
            2,
            (heads,),
            [hs, ts, hs, hs, hs, ps],
            [hs] * whole + [tail],
            [pltpu.VMEM((rows, HEAD_SIZE), jnp.float32)] * 2,
        ),
        out_shape=[out] * whole
        + [jax.ShapeDtypeStruct((3, moving, tails * HEAD_SIZE), jnp.bfloat16)],
        compiler_params=room(20),
        cost_estimate=cost(
            8 * rows * keys * heads * HEAD_SIZE,
            19 * rows * heads * HEAD_SIZE + 2 * heads * rows * keys,
        ),
        name="backward",
    )(here, ids, q, kt, v, g, o, p)


def settle(here, counts, first, local, arrived):
    return pl.pallas_call(
        functools.partial(settle_kernel, first * HEAD_SIZE),
        grid_spec=prefetched(
            2,
            (1,),
            [ANY] * 3 + [pl.BlockSpec(memory_space=pltpu.VMEM)],
            [ANY] * 3,
            [pltpu.SemaphoreType.DMA((3, MOVABLE))],
        ),
        out_shape=[jax.ShapeDtypeStruct(x.shape, x.dtype) for x in local],
        input_output_aliases={2 + i: i for i in range(3)},
        compiler_params=room(8),
        cost_estimate=cost(0, 4 * arrived.size),
        name="settle",
    )(here, counts, *local, arrived)


def project_kernel(turns, final, here_ref, *refs):
    count = 2 * len(turns)
    pieces, w_ref = refs[:count], refs[count]
    out_ref, acc = refs[-2:]
    step = pl.program_id(0)
    part = dot(jnp.concatenate([ref[...] for ref in pieces], axis=0), w_ref[...], (1, 1))

    @pl.when(step == 0)
    def _():
        acc[...] = refs[count + 1][...] + part if final else part

    @pl.when(step > 0)
    def _():
        acc[...] += part

    @pl.when(step == pl.num_programs(0) - 1)
    def _():
        if not final:
            out_ref[...] = acc[...]
            return
        chip, core = here_ref[1], here_ref[2]
        for i in range(count):
            block = core if i % 2 == 0 else 1 - core
            if len(turns) > 1:
                block += 2 * lax.rem(chip + CHIPS - turns[i // 2], CHIPS)
            out_ref[block_at(block), :] = acc[i * BLOCK : (i + 1) * BLOCK].astype(jnp.bfloat16)


def piece_specs(pieces, first, width):
    def spec(x):
        at = first // width if x.shape[1] > pieces[-1].shape[1] else 0
        return pl.BlockSpec((x.shape[0], width), lambda j, *_: (0, at + j))

    return [spec(x) for x in pieces]


def in_hbm(x):
    return pltpu.with_memory_space_constraint(x, pltpu.HBM)


def project(here, turns, pieces, first, width, w, partial, before):
    pieces = [x for t in turns for x in pieces[2 * t : 2 * t + 2]]
    depth = pieces[-1].shape[1]
    rows = sum(x.shape[0] for x in pieces)
    inner = w.shape[0]
    at, place = first // width, turns[0] * 2 * BLOCK // rows
    final = partial is not None
    in_specs = piece_specs(pieces, first, width)
    in_specs.append(pl.BlockSpec((inner, width), lambda j, *_: (0, at + j)))
    operands = [*pieces, w if before is not None else in_hbm(w)]
    aliases = {}
    total = rows
    out_spec = pl.BlockSpec((rows, inner), lambda j, *_: (0, 0))
    if final:
        total = partial.shape[0]
        in_specs.append(pl.BlockSpec((rows, inner), lambda j, *_: (place, 0)))
        operands.append(partial)
        out_spec = pl.BlockSpec((total, inner), lambda j, *_: (0, 0))
    if before is not None:
        in_specs.append(ANY)
        operands.append(before)
        aliases = {len(operands): 0}
        out_spec = pl.BlockSpec(
            (rows, inner), lambda j, here: (lax.rem(here[1] + CHIPS - turns[0], CHIPS), 0)
        )
    return pl.pallas_call(
        functools.partial(project_kernel, turns, final),
        grid_spec=prefetched(
            1, (depth // width,), in_specs, out_spec, [pltpu.VMEM((rows, inner), jnp.float32)]
        ),
        out_shape=jax.ShapeDtypeStruct((total, inner), jnp.bfloat16)
        if final
        else pltpu.HBM((total, inner), jnp.float32),
        input_output_aliases=aliases,
        compiler_params=room(30),
        cost_estimate=cost(
            2 * rows * depth * inner, 2 * rows * depth + 2 * inner * depth + 8 * rows * inner
        ),
        name="project",
    )(here, *operands)


def weight_kernel(here_ref, *refs):
    pieces, h_ref, out_ref = refs[: 2 * CHIPS], refs[2 * CHIPS], refs[-1]
    g = jnp.concatenate([ref[...] for ref in pieces], axis=0)
    term = (dot(g, h_ref[...], (0, 0)) * (1.0 / REPLICAS)).astype(jnp.bfloat16)
    out_ref[...] = term.reshape(out_ref.shape)


def weight(here, pieces, first, width, h):
    depth = pieces[2].shape[1]
    rows, inner = h.shape
    in_specs = piece_specs(pieces, first, width)
    in_specs.append(pl.BlockSpec((rows, inner), lambda j, *_: (0, 0)))
    return pl.pallas_call(
        weight_kernel,
        grid_spec=prefetched(
            1,
            (depth // width,),
            in_specs,
            pl.BlockSpec((16 * width // depth, depth // 16, inner), lambda j, *_: (j, 0, 0)),
        ),
        out_shape=pltpu.HBM((16, depth // 16, inner), jnp.bfloat16),
        compiler_params=room(26),
        cost_estimate=cost(
            2 * rows * depth * inner, 2 * rows * depth + 2 * depth * inner + 2 * rows * inner
        ),
        name="weight",
    )(here, *pieces, h)


def after(x, *others):
    return lax.optimization_barrier((x, *others))[0]


def steps(queries, keys, values, out_gradient, out_weight, segments, counts):
    depth = out_gradient.shape[1]
    half = depth // 2
    here = jnp.stack([lax.axis_index(DP), lax.axis_index("z_lo"), lax.axis_index("core")])
    here = here.astype(jnp.int32)
    ring = [(i, (i + 1) % CHIPS) for i in range(CHIPS)]

    partner = swapped(out_gradient, "core")
    pieces = [[out_gradient, partner] for _ in range(2)]

    def turn(c, x):
        y = lax.ppermute(x, "z_lo", ring)
        z = swapped(y, "core")
        pieces[c] += [y, z]
        return y

    first = turn(0, lax.slice_in_dim(out_gradient, 0, half, axis=1))
    later = lax.slice_in_dim(after(out_gradient, first), half, depth, axis=1)
    second = turn(0, first)
    turn(0, second)
    x = after(later, second)
    for _ in range(3):
        x = turn(1, x)

    chances, head_output, output_turned, keys_turned = forward(here, segments, queries, keys, values)

    partial = project(here, (0, 1, 2, 3), pieces[0], 0, 1280, out_weight, None, None)
    gradient = project(here, (0, 1, 2), pieces[1], half, 1280, out_weight, partial, None)
    gradient = project(here, (3,), pieces[1], half, 1280, out_weight, partial, gradient)

    sums = []
    for c in range(2):
        tiles = weight(here, pieces[c], c * half, 1280, output_turned)
        tiles = lax.all_to_all(tiles, ("y", "x"), 0, 0, tiled=True)
        sums.append(jnp.sum(tiles.astype(jnp.float32), axis=0))
    upper = lax.axis_index("z_hi") == 1
    kept = jnp.where(upper, sums[1], sums[0])
    sent = jnp.where(upper, sums[0], sums[1]).astype(jnp.bfloat16)
    got = swapped(sent, "z_hi")
    weight_gradient = kept + got.astype(jnp.float32)

    heads = queries.shape[1] // HEAD_SIZE
    saved = (queries, keys_turned, values, gradient, head_output, chances)
    (tail_first,) = backward(here, segments, heads - 1, True, *saved)
    arrived_first = swapped(tail_first, "z_hi")
    *local, tail_last = backward(here, segments, heads, False, *saved)
    arrived_last = swapped(tail_last, "z_hi")
    local = settle(here, counts, 0, local, arrived_first)
    local = settle(here, counts, heads - 1, local, arrived_last)
    return (*local, weight_gradient)


def solution(mesh):
    split = Mesh(mesh.devices.reshape(2, 4, 4, CHIPS, 2), AXES)
    placed = (
        P(DP, TENSOR),
        P(DP, TENSOR),
        P(DP, TENSOR),
        P(AXES, None),
        P(TENSOR, None),
        P(),
        P(),
    )
    return jax.shard_map(
        steps,
        mesh=split,
        in_specs=placed,
        out_specs=(P(DP, TENSOR), P(DP, TENSOR), P(DP, TENSOR), P(DP, TENSOR)),
        check_vma=False,
    )
```
